512 devices in a mesh: ka: 128 (over x_lo, z, y), ga: 4 (over x_hi, core).
Axes of the slice: x: 4 (x_hi: 2, x_lo: 2; x = x_hi * 2 + x_lo), y: 8, z: 8, core: 2. Of those that a mesh axis runs over, the one named last changes fastest.
Arguments:
- cond_pairs: bfloat16 [4, 768, 2, 16, 1024], P(None, 'ka', None, None, 'ga'), may hold values from -1 to 1
- val_pairs: bfloat16 [4, 768, 2, 16, 1024], P(None, 'ka', None, None, 'ga'), may hold values from -1 to 1
- screened: bfloat16 [4, 2, 1024, 1024], P(None, None, 'ka', 'ga'), may hold values from -1 to 4, as said below
- k_plus: int32 [4, 768], replicated, may hold values from 0 to 767, as said below
Outputs:
- kernel_forward: float32 [4, 768, 2, 256], P(None, 'ka', None, 'ga')
- kernel_back: float32 [4, 768, 2, 256], P(None, 'ka', None, 'ga')
The draws below stay inside these ranges and needn't reach their ends.
Inputs may be any that keep to these rules, and one draw needn't show every extreme that they name: screened[q, 0] is symmetric and screened[q, 1] antisymmetric in the last two dimensions, so W(q) is Hermitian. For each q there is one translation (dx, dy) of the periodic 64 x 12 grid, with k = x * 12 + y, such that k_plus[q, k] = ((x + dx) mod 64) * 12 + (y + dy) mod 12.
All inputs are finite; a program needn't handle non-finite values.
Results may differ from the reference program's by a relative error of at most 0.0029.
Values may be sent and summed in bfloat16 or wider, within the bound.
No kernel may reach another device: no remote copies, remote signals or barrier semaphores. Data moves between devices by JAX's collectives and lax.ppermute only.
A program may use at most 64 MiB of HBM per device.

```python
import jax
import jax.numpy as jnp
from jax import lax

NG = 1024
Q = 4
K_DEV = 6
CPAIR = 16
VPAIR = 16
KY = 12
KX = 64
NK = 768
N_KA = 128


def draw_screened(key, part):
    base = jax.random.fold_in(key, 7)
    diag_key, real_key, imag_key = jax.random.split(base, 3)
    diagonal = jnp.exp(jax.random.uniform(diag_key, (Q, NG), jnp.float32, -0.7, 0.7))
    raw_real = jax.random.truncated_normal(real_key, -4.0, 4.0, (Q, NG, NG), jnp.float32)
    raw_imag = jax.random.truncated_normal(imag_key, -4.0, 4.0, (Q, NG, NG), jnp.float32)
    factor = 0.35 / jnp.sqrt(jnp.float32(NG))
    identity_grid = jnp.eye(NG, dtype=jnp.float32)
    real_part = (raw_real + jnp.swapaxes(raw_real, 1, 2)) * factor + diagonal[:, :, None] * identity_grid[None]
    imag_part = (raw_imag - jnp.swapaxes(raw_imag, 1, 2)) * factor
    return jnp.stack([real_part, imag_part], 1).astype(jnp.bfloat16)


def draw_k_plus(key, part):
    base = jax.random.fold_in(key, 13)
    row_key, col_key = jax.random.split(base)
    row_step = jax.random.randint(row_key, (Q,), 1, KX)
    col_step = jax.random.randint(col_key, (Q,), 1, KY)
    points = jnp.arange(NK, dtype=jnp.int32)
    grid_row = points // KY
    grid_col = points % KY
    new_row = (grid_row[None, :] + row_step[:, None]) % KX
    new_col = (grid_col[None, :] + col_step[:, None]) % KY
    return (new_row * KY + new_col).astype(jnp.int32)


def levels(stream_key, shape, shards, least, high):
    def one(position, parts):
        draws = jax.random.uniform(jax.random.fold_in(jax.random.fold_in(stream_key, 6), position), (parts,), jnp.float32, least / len(shards), high / len(shards))
        return jnp.repeat(jnp.exp(draws), shape[position] // parts).reshape((-1,) + (1,) * (len(shape) - position - 1))

    loudness = one(*shards[0])
    for cut in shards[1:]:
        loudness = loudness * one(*cut)
    return loudness


def normal_values(rng, extent, scale, most, pieces=(), kind=jnp.bfloat16):
    drawn = scale * jax.random.normal(rng, extent, jnp.float32)
    if pieces:
        drawn = drawn * levels(rng, extent, pieces, -0.22, 0.18)
    return jnp.clip(drawn, -most, most).astype(kind)


def setup_inputs(seed: int = 0) -> dict:
    arg_keys = jax.random.split(jax.random.key(seed), 5)
    cond_pairs = normal_values(arg_keys[0], (Q, NK, 2, CPAIR, NG), (1.0 / NG ** 0.25), 1.0, ((1, 128), (4, 4)))
    val_pairs = normal_values(arg_keys[1], (Q, NK, 2, VPAIR, NG), (1.0 / NG ** 0.25), 1.0, ((1, 128), (4, 4)))
    screened = draw_screened(jax.random.fold_in(arg_keys[4], 71), 0)
    k_plus = draw_k_plus(jax.random.fold_in(arg_keys[4], 71), 0)
    return dict(cond_pairs=cond_pairs, val_pairs=val_pairs, screened=screened, k_plus=k_plus)


def pair_einsum(left, right):
    return jnp.einsum("kag,kbg->kab", left, right)


def block_kernel(cond, val, w_real, w_imag):
    count = cond.shape[0]
    left_real = cond[:, 0].reshape(count * CPAIR, NG)
    left_imag = cond[:, 1].reshape(count * CPAIR, NG)
    real_x = jnp.dot(left_real, w_real, preferred_element_type=jnp.float32) + jnp.dot(left_imag, w_imag, preferred_element_type=jnp.float32)
    imag_x = jnp.dot(left_real, w_imag, preferred_element_type=jnp.float32) - jnp.dot(left_imag, w_real, preferred_element_type=jnp.float32)
    real_b = lax.optimization_barrier(real_x.astype(jnp.bfloat16)).astype(jnp.float32).reshape(count, CPAIR, NG)
    imag_b = lax.optimization_barrier(imag_x.astype(jnp.bfloat16)).astype(jnp.float32).reshape(count, CPAIR, NG)
    val_real = val[:, 0].astype(jnp.float32)
    val_imag = val[:, 1].astype(jnp.float32)
    kernel_real = pair_einsum(real_b, val_real) - pair_einsum(imag_b, val_imag)
    kernel_imag = pair_einsum(real_b, val_imag) + pair_einsum(imag_b, val_real)
    return jnp.stack([kernel_real, kernel_imag], 1).reshape(count, 2, CPAIR * VPAIR)


def reference(cond_pairs, val_pairs, screened, k_plus):
    forwards = []
    backs = []
    for q_index in range(Q):
        cond = cond_pairs[q_index].reshape(N_KA, K_DEV, 2, CPAIR, NG)
        val = val_pairs[q_index].reshape(N_KA, K_DEV, 2, VPAIR, NG)
        w_real = screened[q_index, 0]
        w_imag = screened[q_index, 1]
        blocks = lax.map(lambda both: block_kernel(both[0], both[1], w_real, w_imag), (cond, val))
        forward = blocks.reshape(NK, 2, CPAIR * VPAIR)
        source = jnp.zeros((NK,), jnp.int32).at[k_plus[q_index].astype(jnp.int32)].set(jnp.arange(NK, dtype=jnp.int32))
        forwards.append(forward)
        backs.append(forward[source])
    return jnp.stack(forwards, 0), jnp.stack(backs, 0)
```

```python
import functools

import jax
import jax.numpy as jnp
from jax import lax
from jax.experimental import pallas as pl
from jax.experimental.pallas import tpu as pltpu
from jax.sharding import Mesh
from jax.sharding import PartitionSpec as P

NG = 1024
Q = 4
PAIR = 16
BLK = 128
NB = NG // BLK
SENT = 5
KQ = 6
BF = jnp.bfloat16
F32 = jnp.float32


def nt(left, right, precision=None):
    return lax.dot_general(
        left, right, (((1,), (1,)), ((), ())), preferred_element_type=F32, precision=precision
    )


def nn(left, right, precision=None):
    return jnp.dot(left, right, preferred_element_type=F32, precision=precision)


def contract(sign_ref, left_ref, val_ref, own_ref, oth_ref, out_ref, p_ref, q_ref):
    sign = sign_ref[0].astype(BF)
    left = left_ref[...]
    flipped = left * sign
    rows = left.shape[0]
    wrapped = jnp.concatenate([left, left[:, : 3 * BLK]], 1)
    wrapped_flip = jnp.concatenate([flipped, flipped[:, : 3 * BLK]], 1)
    for b in range(NB):
        lo, hi = b * BLK, (b + 1) * BLK
        far = wrapped[:, hi : hi + 3 * BLK]
        far_flip = wrapped_flip[:, hi : hi + 3 * BLK]
        own = own_ref[lo:hi, :]
        oth = oth_ref[lo:hi, :]
        p_back = nt(far_flip, own[:, BLK : 4 * BLK])
        q_back = -nt(far, oth[:, BLK : 4 * BLK])
        if b == 0:
            p_ref[...] = jnp.zeros_like(p_ref)
            q_ref[...] = jnp.zeros_like(q_ref)
        p_ref[:, lo:hi] += p_back
        q_ref[:, lo:hi] += q_back
        p_fore = nn(left[:, lo:hi], own)
        q_fore = nn(flipped[:, lo:hi], oth)
        first = min(SENT, NB - b)
        p_ref[:, lo : lo + first * BLK] += p_fore[:, : first * BLK]
        q_ref[:, lo : lo + first * BLK] += q_fore[:, : first * BLK]
        if first < SENT:
            p_ref[:, : (SENT - first) * BLK] += p_fore[:, first * BLK :]
            q_ref[:, : (SENT - first) * BLK] += q_fore[:, first * BLK :]
    p = p_ref[...].reshape(KQ, 2, PAIR, NG)
    q = q_ref[...].reshape(KQ, 2, PAIR, NG)
    half = rows // 2
    x_real = (p[:, 0] + q[:, 1]).reshape(half, NG).astype(BF)
    x_imag = (q[:, 0] - p[:, 1]).reshape(half, NG).astype(BF)
    val = val_ref[...]
    g1 = nt(x_real, val)
    g2 = nt(x_imag, val)
    r = lax.broadcasted_iota(jnp.int32, (half, rows), 0)
    c = lax.broadcasted_iota(jnp.int32, (half, rows), 1)
    same = r // PAIR == c // (2 * PAIR)
    g1 = jnp.where(same, g1, 0.0)
    g2 = jnp.where(same, g2, 0.0)
    c = lax.broadcasted_iota(jnp.int32, (rows, 128), 0)
    l = lax.broadcasted_iota(jnp.int32, (rows, 128), 1)
    hit = c % PAIR == l % PAIR
    part = (c // PAIR) % 2
    want = l // 64
    e1 = jnp.where(hit & (part == want), 1.0, 0.0)
    e2 = jnp.where(hit & (part != want), jnp.where(want == 0, -1.0, 1.0), 0.0)
    t = nn(g1, e1, lax.Precision.HIGHEST) + nn(g2, e2, lax.Precision.HIGHEST)
    r = lax.broadcasted_iota(jnp.int32, (half, 128), 0)
    l = lax.broadcasted_iota(jnp.int32, (half, 128), 1)
    t = jnp.where(r % 4 == (l // PAIR) % 4, t, 0.0)
    o = lax.broadcasted_iota(jnp.int32, (4 * KQ, half), 0)
    r = lax.broadcasted_iota(jnp.int32, (4 * KQ, half), 1)
    e3 = jnp.where((r // PAIR == o % KQ) & ((r % PAIR) // 4 == o // KQ), 1.0, 0.0)
    out_ref[...] = nn(e3, t, lax.Precision.HIGHEST)


def contracted(sign, left, val, own, oth):
    vm = pl.BlockSpec(memory_space=pltpu.VMEM)
    return pl.pallas_call(
        contract,
        out_shape=jax.ShapeDtypeStruct((4 * KQ, 128), F32),
        in_specs=[pl.BlockSpec(memory_space=pltpu.SMEM), vm, vm, vm, vm],
        out_specs=vm,
        scratch_shapes=[
            pltpu.VMEM((2 * KQ * PAIR, NG), F32),
            pltpu.VMEM((2 * KQ * PAIR, NG), F32),
        ],
        cost_estimate=pl.CostEstimate(
            flops=1_600_000_000, bytes_accessed=4_000_000, transcendentals=0
        ),
    )(sign, left, val, own, oth)


def pick_rows(at_ref, got_ref, fwd_ref, pay_ref):
    xl = at_ref[0]
    yl = at_ref[1]
    for q in range(Q):
        base = (q // 2) * 8 + (q % 2) * 2
        other = at_ref[2 + q]
        begin = at_ref[6 + q]
        for t in range(KQ):
            fwd_ref[q, pl.ds(t, 1), :] = got_ref[base + yl * 4 + t // 3, pl.ds(xl * 3 + t % 3, 1), :]
            col = lax.rem(begin + t, 12)
            slot = base + (col // 6) * 4 + (col % 6) // 3
            pay_ref[pl.ds(q * KQ + t, 1), :] = got_ref[slot, pl.ds(other * 3 + col % 3, 1), :]


def pick_back(at_ref, got_ref, out_ref):
    for q in range(Q):
        out_ref[q, :, :] = got_ref[at_ref[q], q * KQ : (q + 1) * KQ, :]


def local(cond, val, screened, k_plus):
    xl, yl, core = lax.axis_index("xl"), lax.axis_index("yl"), lax.axis_index("c")
    z, yh = lax.axis_index("z"), lax.axis_index("yh")
    row8 = ("xl", "xh", "c")
    w = lax.all_to_all(screened.reshape(8, 8, 256), row8, 0, 0)
    w = jnp.transpose(w.reshape(2, 4, 8, 256), (0, 2, 1, 3)).reshape(2, 8, NG)
    w = jnp.concatenate([w, w[:, :, : 4 * BLK]], 2)
    cut = [
        lax.dynamic_slice_in_dim(w[i], (4 * i + z // 2) * BLK, SENT * BLK, 1) for i in range(2)
    ]
    w = jnp.stack(cut, 0)
    w = lax.all_to_all(jnp.broadcast_to(w, (64,) + w.shape), ("z", "yh", "yl"), 0, 0)
    own = jnp.transpose(w, (1, 0, 2, 3)).reshape(NG, SENT * BLK)
    oth = lax.ppermute(own, "c", [(0, 1), (1, 0)])

    def spread(pairs):
        got = lax.all_to_all(pairs.reshape(8, 3, 2, PAIR, 256), row8, 0, 0)
        return jnp.transpose(got.reshape(2, 4, 3, 2, PAIR, 256), (0, 2, 3, 4, 1, 5)).reshape(
            KQ, 2, PAIR, NG
        )

    left = spread(cond)
    left = jnp.where(core == 0, left, jnp.stack([left[:, 1], -left[:, 0]], 1))
    right = spread(val)
    sign = jnp.where(core == 0, 1.0, -1.0).astype(F32).reshape(1)
    block = contracted(
        sign, left.reshape(2 * KQ * PAIR, NG), right.reshape(2 * KQ * PAIR, NG), own, oth
    )
    slots = jnp.broadcast_to(block.reshape(1, 1, 4, KQ, 128), (2, 2, 4, KQ, 128))
    got = lax.all_to_all(slots.reshape(16, KQ, 128), ("xl", "yl", "xh", "c"), 0, 0)
    corner = k_plus[:, 0]
    row_step, col_step = corner // 12, corner % 12
    here = z * 4 + yh
    other = xl ^ ((here + row_step) // 32 % 2)
    begin = (6 * yl - col_step + 12) % 12
    at = jnp.concatenate([jnp.stack([xl, yl]), other, begin]).astype(jnp.int32)
    vm = pl.BlockSpec(memory_space=pltpu.VMEM)
    sm = pl.BlockSpec(memory_space=pltpu.SMEM)
    forward, pay = pl.pallas_call(
        pick_rows,
        out_shape=(
            jax.ShapeDtypeStruct((Q, KQ, 128), F32),
            jax.ShapeDtypeStruct((Q * KQ, 128), F32),
        ),
        in_specs=[sm, vm],
        out_specs=(vm, vm),
    )(at, got)
    came = lax.all_to_all(jnp.broadcast_to(pay, (32,) + pay.shape), ("z", "yh"), 0, 0)
    source = ((here - row_step) % 32).astype(jnp.int32)
    back = pl.pallas_call(
        pick_back,
        out_shape=jax.ShapeDtypeStruct((Q, KQ, 128), F32),
        in_specs=[sm, vm],
        out_specs=vm,
    )(source, came)
    return forward.reshape(Q, KQ, 2, 64), back.reshape(Q, KQ, 2, 64)


def solution(mesh):
    fine = Mesh(mesh.devices.reshape(2, 8, 4, 2, 2, 2), ("xl", "z", "yh", "yl", "xh", "c"))
    ka, ga = ("xl", "z", "yh", "yl"), ("xh", "c")
    in_specs = (
        P(None, ka, None, None, ga),
        P(None, ka, None, None, ga),
        P(None, None, ka, ga),
        P(),
    )
    out_specs = (P(None, ka, None, ga), P(None, ka, None, ga))
    return jax.shard_map(local, mesh=fine, in_specs=in_specs, out_specs=out_specs, check_vma=False)
```

```python
import jax
import jax.numpy as jnp
from jax import lax
from jax.experimental import pallas as pl
from jax.experimental.pallas import tpu as pltpu
from jax.sharding import Mesh
from jax.sharding import PartitionSpec as P

NG = 1024
Q = 4
PAIR = 16
BLK = 128
NB = NG // BLK
SENT = 5
KQ = 6
BF = jnp.bfloat16
F32 = jnp.float32


def nt(left, right, precision=None):
    return lax.dot_general(
        left, right, (((1,), (1,)), ((), ())), preferred_element_type=F32, precision=precision
    )


def nn(left, right, precision=None):
    return jnp.dot(left, right, preferred_element_type=F32, precision=precision)


def assemble(at_ref, *refs):
    pieces, (left_ref, flip_ref, val_ref) = refs[:8], refs[8:]
    x, core = at_ref[0], at_ref[1]
    minus = jnp.where(core == 0, 1.0, -1.0).astype(BF)
    for s in range(4):
        xl = (x ^ s) // 2
        for t in range(2):
            g = ((x ^ s) % 2) * 2 + (core ^ t)
            lanes = pl.ds(pl.multiple_of(g * 256, 256), 256)
            for j in range(3):
                row = xl * 96 + j * 32
                whole = pl.ds(pl.multiple_of(row, 32), 32)
                val_ref[whole, lanes] = pieces[4 + s][t, j].reshape(32, 256)
                for r in range(2):
                    part = pl.ds(pl.multiple_of(row + (r ^ core) * PAIR, PAIR), PAIR)
                    piece = pieces[s][t, j, r]
                    if r == 0:
                        piece = piece * minus
                    left_ref[part, lanes] = piece
                    flip_ref[part, lanes] = piece * minus


def assembled(at, pieces):
    vm = pl.BlockSpec(memory_space=pltpu.VMEM)
    flat = jax.ShapeDtypeStruct((2 * KQ * PAIR, NG), BF)
    return pl.pallas_call(
        assemble,
        out_shape=(flat, flat, flat),
        in_specs=[pl.BlockSpec(memory_space=pltpu.SMEM)] + [vm] * 8,
        out_specs=(vm, vm, vm),
        cost_estimate=pl.CostEstimate(flops=0, bytes_accessed=2_000_000, transcendentals=0),
    )(at, *pieces)


def contract(left_ref, flip_ref, val_ref, own_ref, oth_ref, out_ref, p_ref, q_ref):
    left = left_ref[...]
    flipped = flip_ref[...]
    rows = left.shape[0]
    wrapped = jnp.concatenate([left, left[:, : 3 * BLK]], 1)
    wrapped_flip = jnp.concatenate([flipped, flipped[:, : 3 * BLK]], 1)
    for b in range(NB):
        lo, hi = b * BLK, (b + 1) * BLK
        far = wrapped[:, hi : hi + 3 * BLK]
        far_flip = wrapped_flip[:, hi : hi + 3 * BLK]
        own = own_ref[lo:hi, :]
        oth = oth_ref[lo:hi, :]
        p_back = nt(far_flip, own[:, BLK : 4 * BLK])
        q_back = -nt(far, oth[:, BLK : 4 * BLK])
        if b == 0:
            p_ref[...] = jnp.zeros_like(p_ref)
            q_ref[...] = jnp.zeros_like(q_ref)
        p_ref[:, lo:hi] += p_back
        q_ref[:, lo:hi] += q_back
        p_fore = nn(left[:, lo:hi], own)
        q_fore = nn(flipped[:, lo:hi], oth)
        first = min(SENT, NB - b)
        p_ref[:, lo : lo + first * BLK] += p_fore[:, : first * BLK]
        q_ref[:, lo : lo + first * BLK] += q_fore[:, : first * BLK]
        if first < SENT:
            p_ref[:, : (SENT - first) * BLK] += p_fore[:, first * BLK :]
            q_ref[:, : (SENT - first) * BLK] += q_fore[:, first * BLK :]
    p = p_ref[...].reshape(KQ, 2, PAIR, NG)
    q = q_ref[...].reshape(KQ, 2, PAIR, NG)
    half = rows // 2
    x_real = (p[:, 0] + q[:, 1]).reshape(half, NG).astype(BF)
    x_imag = (q[:, 0] - p[:, 1]).reshape(half, NG).astype(BF)
    val = val_ref[...]
    g1 = nt(x_real, val)
    g2 = nt(x_imag, val)
    r = lax.broadcasted_iota(jnp.int32, (half, rows), 0)
    c = lax.broadcasted_iota(jnp.int32, (half, rows), 1)
    same = r // PAIR == c // (2 * PAIR)
    g1 = jnp.where(same, g1, 0.0)
    g2 = jnp.where(same, g2, 0.0)
    c = lax.broadcasted_iota(jnp.int32, (rows, 128), 0)
    l = lax.broadcasted_iota(jnp.int32, (rows, 128), 1)
    hit = c % PAIR == l % PAIR
    part = (c // PAIR) % 2
    want = l // 64
    e1 = jnp.where(hit & (part == want), 1.0, 0.0)
    e2 = jnp.where(hit & (part != want), jnp.where(want == 0, -1.0, 1.0), 0.0)
    t = nn(g1, e1, lax.Precision.HIGHEST) + nn(g2, e2, lax.Precision.HIGHEST)
    r = lax.broadcasted_iota(jnp.int32, (half, 128), 0)
    l = lax.broadcasted_iota(jnp.int32, (half, 128), 1)
    t = jnp.where(r % 4 == (l // PAIR) % 4, t, 0.0)
    o = lax.broadcasted_iota(jnp.int32, (4 * 8, half), 0)
    r = lax.broadcasted_iota(jnp.int32, (4 * 8, half), 1)
    e3 = jnp.where((r // PAIR == o % 8) & ((r % PAIR) // 4 == o // 8), 1.0, 0.0)
    block = nn(e3, t, lax.Precision.HIGHEST)
    for slot in range(16):
        g = slot % 4
        out_ref[slot, :, :] = block[g * 8 : g * 8 + KQ, :]


def contracted(left, flipped, val, own, oth):
    vm = pl.BlockSpec(memory_space=pltpu.VMEM)
    return pl.pallas_call(
        contract,
        out_shape=jax.ShapeDtypeStruct((16, KQ, 128), F32),
        in_specs=[vm] * 5,
        out_specs=vm,
        scratch_shapes=[
            pltpu.VMEM((2 * KQ * PAIR, NG), F32),
            pltpu.VMEM((2 * KQ * PAIR, NG), F32),
        ],
        cost_estimate=pl.CostEstimate(
            flops=1_600_000_000, bytes_accessed=4_000_000, transcendentals=0
        ),
    )(left, flipped, val, own, oth)


def pick_rows(at_ref, came_ref, fwd_ref, pay_ref, got_ref, sem):
    copy = pltpu.make_async_copy(came_ref, got_ref, sem)
    copy.start()
    copy.wait()
    xl = at_ref[0]
    yl = at_ref[1]
    for q in range(Q):
        base = (q // 2) * 8 + (q % 2) * 2
        other = at_ref[2 + q]
        begin = at_ref[6 + q]
        for t in range(KQ):
            row = got_ref[base + yl * 4 + t // 3, pl.ds(xl * 3 + t % 3, 1), :]
            fwd_ref[q, pl.ds(t, 1), 0, :] = row[:, :64]
            fwd_ref[q, pl.ds(t, 1), 1, :] = row[:, 64:]
            col = lax.rem(begin + t, 12)
            slot = base + (col // 6) * 4 + (col % 6) // 3
            pay_ref[0, pl.ds(q * KQ + t, 1), :] = got_ref[slot, pl.ds(other * 3 + col % 3, 1), :]
    pay = pay_ref[0]
    for slot in range(1, 32):
        pay_ref[slot, :, :] = pay


def pick_back(at_ref, came_ref, out_ref, got_ref, sem):
    copies = [
        pltpu.make_async_copy(came_ref.at[at_ref[q]], got_ref.at[q], sem.at[q]) for q in range(Q)
    ]
    for copy in copies:
        copy.start()
    for q in range(Q):
        copies[q].wait()
        rows = got_ref[q, q * KQ : (q + 1) * KQ, :]
        out_ref[q, :, 0, :] = rows[:, :64]
        out_ref[q, :, 1, :] = rows[:, 64:]


def local(cond, val, screened, k_plus):
    xl, yl, core = lax.axis_index("xl"), lax.axis_index("yl"), lax.axis_index("c")
    z, yh = lax.axis_index("z"), lax.axis_index("yh")
    row8 = ("xl", "xh", "c")
    w = lax.all_to_all(screened.reshape(8, 8, 256), row8, 0, 0)
    w = jnp.transpose(w.reshape(2, 4, 8, 256), (0, 2, 1, 3)).reshape(2, 8, NG)
    w = jnp.concatenate([w, w[:, :, : 4 * BLK]], 2)
    cut = [
        lax.dynamic_slice_in_dim(w[i], (4 * i + z // 2) * BLK, SENT * BLK, 1) for i in range(2)
    ]
    w = jnp.stack(cut, 0)
    w = jnp.broadcast_to(w, (64,) + w.shape)
    w = lax.all_to_all(w, ("z", "yh", "yl"), 0, 0)
    own = jnp.transpose(w, (1, 0, 2, 3)).reshape(NG, SENT * BLK)
    oth = lax.ppermute(own, "c", [(0, 1), (1, 0)])

    x = xl * 2 + lax.axis_index("xh")

    def spread(pairs):
        slots = pairs.reshape(4, 2, 3, 2, PAIR, 256)
        keep = lax.dynamic_index_in_dim(slots, core, 1, False)
        given = lax.dynamic_index_in_dim(slots, 1 - core, 1, False)
        given = lax.ppermute(given, "c", [(0, 1), (1, 0)])
        pieces = []
        for s in range(4):
            both = [lax.dynamic_index_in_dim(part, x ^ s, 0, True) for part in (keep, given)]
            piece = jnp.concatenate(both, 0)
            if s:
                piece = lax.ppermute(piece, ("xl", "xh"), [(i, i ^ s) for i in range(4)])
            pieces.append(piece)
        return pieces

    pieces = spread(cond) + spread(val)
    here_x = jnp.stack([x, core]).astype(jnp.int32)
    left, flipped, right = assembled(here_x, pieces)
    slots = contracted(left, flipped, right, own, oth)
    got = lax.all_to_all(slots, ("xl", "yl", "xh", "c"), 0, 0)
    corner = k_plus[:, 0]
    row_step, col_step = corner // 12, corner % 12
    here = z * 4 + yh
    other = xl ^ ((here + row_step) // 32 % 2)
    begin = (6 * yl - col_step + 12) % 12
    at = jnp.concatenate([jnp.stack([xl, yl]), other, begin]).astype(jnp.int32)
    vm = pl.BlockSpec(memory_space=pltpu.VMEM)
    sm = pl.BlockSpec(memory_space=pltpu.SMEM)
    anywhere = pl.BlockSpec(memory_space=pl.ANY)
    out = jax.ShapeDtypeStruct((Q, KQ, 2, 64), F32)
    forward, pay = pl.pallas_call(
        pick_rows,
        out_shape=(out, jax.ShapeDtypeStruct((32, Q * KQ, 128), F32)),
        in_specs=[sm, anywhere],
        out_specs=(vm, vm),
        scratch_shapes=[pltpu.VMEM((16, KQ, 128), F32), pltpu.SemaphoreType.DMA],
        compiler_params=pltpu.CompilerParams(vmem_limit_bytes=8 << 20),
    )(at, got)
    came = lax.all_to_all(pay, ("z", "yh"), 0, 0)
    source = ((here - row_step) % 32).astype(jnp.int32)
    back = pl.pallas_call(
        pick_back,
        out_shape=out,
        in_specs=[sm, anywhere],
        out_specs=vm,
        scratch_shapes=[pltpu.VMEM((Q, Q * KQ, 128), F32), pltpu.SemaphoreType.DMA((Q,))],
        compiler_params=pltpu.CompilerParams(vmem_limit_bytes=8 << 20),
    )(source, came)
    return forward, back


def solution(mesh):
    fine = Mesh(mesh.devices.reshape(2, 8, 4, 2, 2, 2), ("xl", "z", "yh", "yl", "xh", "c"))
    ka, ga = ("xl", "z", "yh", "yl"), ("xh", "c")
    in_specs = (
        P(None, ka, None, None, ga),
        P(None, ka, None, None, ga),
        P(None, None, ka, ga),
        P(),
    )
    out_specs = (P(None, ka, None, ga), P(None, ka, None, ga))
    return jax.shard_map(local, mesh=fine, in_specs=in_specs, out_specs=out_specs, check_vma=False)
```

```python
import jax
import jax.numpy as jnp
from jax import lax
from jax.experimental import pallas as pl
from jax.experimental.pallas import tpu as pltpu
from jax.sharding import Mesh
from jax.sharding import PartitionSpec as P

NG = 1024
Q = 4
PAIR = 16
BLK = 128
NB = NG // BLK
SENT = 5
KQ = 6
BF = jnp.bfloat16
F32 = jnp.float32


def nt(left, right, precision=None):
    return lax.dot_general(
        left, right, (((1,), (1,)), ((), ())), preferred_element_type=F32, precision=precision
    )


def nn(left, right, precision=None):
    return jnp.dot(left, right, preferred_element_type=F32, precision=precision)


def assemble(at_ref, *refs):
    pieces, (left_ref, flip_ref, val_ref) = refs[:4], refs[4:]
    x, core = at_ref[0], at_ref[1]
    minus = jnp.where(core == 0, 1.0, -1.0).astype(BF)
    for s in range(4):
        xl = (x ^ s) // 2
        for t in range(2):
            g = ((x ^ s) % 2) * 2 + (core ^ t)
            lanes = pl.ds(pl.multiple_of(g * 256, 256), 256)
            for j in range(3):
                row = xl * 96 + j * 32
                whole = pl.ds(pl.multiple_of(row, 32), 32)
                val_ref[whole, lanes] = pieces[s][1, t, j].reshape(32, 256)
                for r in range(2):
                    part = pl.ds(pl.multiple_of(row + (r ^ core) * PAIR, PAIR), PAIR)
                    piece = pieces[s][0, t, j, r]
                    if r == 0:
                        piece = piece * minus
                    left_ref[part, lanes] = piece
                    flip_ref[part, lanes] = piece * minus


def assembled(at, pieces):
    vm = pl.BlockSpec(memory_space=pltpu.VMEM)
    flat = jax.ShapeDtypeStruct((2 * KQ * PAIR, NG), BF)
    return pl.pallas_call(
        assemble,
        out_shape=(flat, flat, flat),
        in_specs=[pl.BlockSpec(memory_space=pltpu.SMEM)] + [vm] * 4,
        out_specs=(vm, vm, vm),
        cost_estimate=pl.CostEstimate(flops=0, bytes_accessed=2_000_000, transcendentals=0),
    )(at, *pieces)


def screen(ahead_ref, behind_ref, w_ref, sum_ref, negate):
    ahead = ahead_ref[...]
    behind = behind_ref[...]
    wrapped = jnp.concatenate([behind, behind[:, : 3 * BLK]], 1)
    sum_ref[...] = jnp.zeros_like(sum_ref)
    for b in range(NB):
        lo, hi = b * BLK, (b + 1) * BLK
        w = w_ref[lo:hi, :]
        back = nt(wrapped[:, hi : hi + 3 * BLK], w[:, BLK : 4 * BLK])
        sum_ref[:, lo:hi] += -back if negate else back
        fore = nn(ahead[:, lo:hi], w)
        first = min(SENT, NB - b)
        sum_ref[:, lo : lo + first * BLK] += fore[:, : first * BLK]
        if first < SENT:
            sum_ref[:, : (SENT - first) * BLK] += fore[:, first * BLK :]


def contract_own(left_ref, flip_ref, own_ref, p_ref):
    screen(left_ref, flip_ref, own_ref, p_ref, False)


def contract(left_ref, flip_ref, val_ref, oth_ref, p_ref, out_ref, q_ref):
    screen(flip_ref, left_ref, oth_ref, q_ref, True)
    rows = left_ref.shape[0]
    p = p_ref[...].reshape(KQ, 2, PAIR, NG)
    q = q_ref[...].reshape(KQ, 2, PAIR, NG)
    half = rows // 2
    x_real = (p[:, 0] + q[:, 1]).reshape(half, NG).astype(BF)
    x_imag = (q[:, 0] - p[:, 1]).reshape(half, NG).astype(BF)
    val = val_ref[...]
    g1 = nt(x_real, val)
    g2 = nt(x_imag, val)
    r = lax.broadcasted_iota(jnp.int32, (half, rows), 0)
    c = lax.broadcasted_iota(jnp.int32, (half, rows), 1)
    same = r // PAIR == c // (2 * PAIR)
    g1 = jnp.where(same, g1, 0.0)
    g2 = jnp.where(same, g2, 0.0)
    c = lax.broadcasted_iota(jnp.int32, (rows, 128), 0)
    l = lax.broadcasted_iota(jnp.int32, (rows, 128), 1)
    hit = c % PAIR == l % PAIR
    part = (c // PAIR) % 2
    want = l // 64
    e1 = jnp.where(hit & (part == want), 1.0, 0.0)
    e2 = jnp.where(hit & (part != want), jnp.where(want == 0, -1.0, 1.0), 0.0)
    t = nn(g1, e1, lax.Precision.HIGHEST) + nn(g2, e2, lax.Precision.HIGHEST)
    r = lax.broadcasted_iota(jnp.int32, (half, 128), 0)
    l = lax.broadcasted_iota(jnp.int32, (half, 128), 1)
    t = jnp.where(r % 4 == (l // PAIR) % 4, t, 0.0)
    o = lax.broadcasted_iota(jnp.int32, (4 * 8, half), 0)
    r = lax.broadcasted_iota(jnp.int32, (4 * 8, half), 1)
    e3 = jnp.where((r // PAIR == o % 8) & ((r % PAIR) // 4 == o // 8), 1.0, 0.0)
    block = nn(e3, t, lax.Precision.HIGHEST)
    for slot in range(16):
        g = slot % 4
        out_ref[slot, :, :] = block[g * 8 : g * 8 + KQ, :]


def contracted(left, flipped, val, own, oth):
    vm = pl.BlockSpec(memory_space=pltpu.VMEM)
    cost = pl.CostEstimate(flops=800_000_000, bytes_accessed=3_000_000, transcendentals=0)
    sums = (2 * KQ * PAIR, NG)
    p = pl.pallas_call(
        contract_own,
        out_shape=jax.ShapeDtypeStruct(sums, F32),
        in_specs=[vm] * 3,
        out_specs=vm,
        cost_estimate=cost,
    )(left, flipped, own)
    return pl.pallas_call(
        contract,
        out_shape=jax.ShapeDtypeStruct((16, KQ, 128), F32),
        in_specs=[vm] * 5,
        out_specs=vm,
        scratch_shapes=[pltpu.VMEM(sums, F32)],
        cost_estimate=cost,
    )(left, flipped, val, oth, p)


def pick_rows(at_ref, came_ref, fwd_ref, pay_ref, got_ref, sem):
    copy = pltpu.make_async_copy(came_ref, got_ref, sem)
    copy.start()
    copy.wait()
    xl = at_ref[0]
    yl = at_ref[1]
    for q in range(Q):
        base = (q // 2) * 8 + (q % 2) * 2
        other = at_ref[2 + q]
        begin = at_ref[6 + q]
        for t in range(KQ):
            row = got_ref[base + yl * 4 + t // 3, pl.ds(xl * 3 + t % 3, 1), :]
            fwd_ref[q, pl.ds(t, 1), 0, :] = row[:, :64]
            fwd_ref[q, pl.ds(t, 1), 1, :] = row[:, 64:]
            col = lax.rem(begin + t, 12)
            slot = base + (col // 6) * 4 + (col % 6) // 3
            pay_ref[0, pl.ds(q * KQ + t, 1), :] = got_ref[slot, pl.ds(other * 3 + col % 3, 1), :]
    pay = pay_ref[0]
    for slot in range(1, 32):
        pay_ref[slot, :, :] = pay


def pick_back(at_ref, came_ref, out_ref, got_ref, sem):
    copies = [
        pltpu.make_async_copy(came_ref.at[at_ref[q]], got_ref.at[q], sem.at[q]) for q in range(Q)
    ]
    for copy in copies:
        copy.start()
    for q in range(Q):
        copies[q].wait()
        rows = got_ref[q, q * KQ : (q + 1) * KQ, :]
        out_ref[q, :, 0, :] = rows[:, :64]
        out_ref[q, :, 1, :] = rows[:, 64:]


def local(cond, val, screened, k_plus):
    xl, yl, core = lax.axis_index("xl"), lax.axis_index("yl"), lax.axis_index("c")
    z, yh = lax.axis_index("z"), lax.axis_index("yh")
    w = screened.reshape(2, 1, 4, 8, 256)
    w = jnp.broadcast_to(w, (2, 2, 4, 8, 256)).reshape(16, 8, 256)
    w = lax.all_to_all(w, ("xl", "yl", "xh", "c"), 0, 0)
    w = jnp.transpose(w.reshape(2, 2, 4, 8, 256), (0, 1, 3, 2, 4)).reshape(2, 2, 8, NG)
    w = jnp.concatenate([w, w[..., : 4 * BLK]], 3)
    cut = [
        lax.dynamic_slice_in_dim(w[i], (4 * i + z // 2) * BLK, SENT * BLK, 2) for i in range(2)
    ]
    w = jnp.stack(cut, 0)
    w = jnp.broadcast_to(w, (32,) + w.shape)
    w = lax.all_to_all(w, ("z", "yh"), 0, 0)
    own = jnp.transpose(w, (1, 0, 2, 3, 4)).reshape(NG, SENT * BLK)
    oth = lax.ppermute(own, "c", [(0, 1), (1, 0)])

    x = xl * 2 + lax.axis_index("xh")

    slots = [pairs.reshape(4, 2, 3, 2, PAIR, 256) for pairs in (cond, val)]
    keep = [lax.dynamic_index_in_dim(part, core, 1, False) for part in slots]
    given = [lax.dynamic_index_in_dim(part, 1 - core, 1, False) for part in slots]
    given = jnp.stack(given, 0)
    given = lax.ppermute(given, "c", [(0, 1), (1, 0)])
    pieces = []
    for s in range(4):
        both = [
            lax.dynamic_index_in_dim(part, x ^ s, 0, False)
            for part in (keep[0], given[0], keep[1], given[1])
        ]
        piece = jnp.stack(both, 0).reshape(2, 2, 3, 2, PAIR, 256)
        if s:
            piece = lax.ppermute(piece, ("xl", "xh"), [(i, i ^ s) for i in range(4)])
        pieces.append(piece)
    here_x = jnp.stack([x, core]).astype(jnp.int32)
    left, flipped, right = assembled(here_x, pieces)
    slots = contracted(left, flipped, right, own, oth)
    got = lax.all_to_all(slots, ("xl", "yl", "xh", "c"), 0, 0)
    corner = k_plus[:, 0]
    row_step, col_step = corner // 12, corner % 12
    here = z * 4 + yh
    other = xl ^ ((here + row_step) // 32 % 2)
    begin = (6 * yl - col_step + 12) % 12
    at = jnp.concatenate([jnp.stack([xl, yl]), other, begin]).astype(jnp.int32)
    vm = pl.BlockSpec(memory_space=pltpu.VMEM)
    sm = pl.BlockSpec(memory_space=pltpu.SMEM)
    anywhere = pl.BlockSpec(memory_space=pl.ANY)
    out = jax.ShapeDtypeStruct((Q, KQ, 2, 64), F32)
    forward, pay = pl.pallas_call(
        pick_rows,
        out_shape=(out, jax.ShapeDtypeStruct((32, Q * KQ, 128), F32)),
        in_specs=[sm, anywhere],
        out_specs=(vm, vm),
        scratch_shapes=[pltpu.VMEM((16, KQ, 128), F32), pltpu.SemaphoreType.DMA],
        compiler_params=pltpu.CompilerParams(vmem_limit_bytes=8 << 20),
    )(at, got)
    came = lax.all_to_all(pay, ("z", "yh"), 0, 0)
    source = ((here - row_step) % 32).astype(jnp.int32)
    back = pl.pallas_call(
        pick_back,
        out_shape=out,
        in_specs=[sm, anywhere],
        out_specs=vm,
        scratch_shapes=[pltpu.VMEM((Q, Q * KQ, 128), F32), pltpu.SemaphoreType.DMA((Q,))],
        compiler_params=pltpu.CompilerParams(vmem_limit_bytes=8 << 20),
    )(source, came)
    return forward, back


def solution(mesh):
    fine = Mesh(mesh.devices.reshape(2, 8, 4, 2, 2, 2), ("xl", "z", "yh", "yl", "xh", "c"))
    ka, ga = ("xl", "z", "yh", "yl"), ("xh", "c")
    in_specs = (
        P(None, ka, None, None, ga),
        P(None, ka, None, None, ga),
        P(None, None, ka, ga),
        P(),
    )
    out_specs = (P(None, ka, None, ga), P(None, ka, None, ga))
    return jax.shard_map(local, mesh=fine, in_specs=in_specs, out_specs=out_specs, check_vma=False)
```

```python
import jax
import jax.numpy as jnp
from jax import lax
from jax.experimental import pallas as pl
from jax.experimental.pallas import tpu as pltpu
from jax.sharding import Mesh
from jax.sharding import PartitionSpec as P

NG = 1024
Q = 4
PAIR = 16
BLK = 128
NB = NG // BLK
SENT = 5
KQ = 6
BF = jnp.bfloat16
F32 = jnp.float32


def nt(left, right, precision=None):
    return lax.dot_general(
        left, right, (((1,), (1,)), ((), ())), preferred_element_type=F32, precision=precision
    )


def nn(left, right, precision=None):
    return jnp.dot(left, right, preferred_element_type=F32, precision=precision)


def assemble(at_ref, *refs):
    pieces, (left_ref, flip_ref, val_ref) = refs[:4], refs[4:]
    x, core = at_ref[0], at_ref[1]
    minus = jnp.where(core == 0, 1.0, -1.0).astype(BF)
    for s in range(4):
        xl = (x ^ s) // 2
        for t in range(2):
            g = ((x ^ s) % 2) * 2 + (core ^ t)
            lanes = pl.ds(pl.multiple_of(g * 256, 256), 256)
            for j in range(3):
                row = xl * 96 + j * 32
                whole = pl.ds(pl.multiple_of(row, 32), 32)
                val_ref[whole, lanes] = pieces[s][1, t, j].reshape(32, 256)
                for r in range(2):
                    part = pl.ds(pl.multiple_of(row + (r ^ core) * PAIR, PAIR), PAIR)
                    piece = pieces[s][0, t, j, r]
                    if r == 0:
                        piece = piece * minus
                    left_ref[part, lanes] = piece
                    flip_ref[part, lanes] = piece * minus


def assembled(at, pieces):
    vm = pl.BlockSpec(memory_space=pltpu.VMEM)
    flat = jax.ShapeDtypeStruct((2 * KQ * PAIR, NG), BF)
    return pl.pallas_call(
        assemble,
        out_shape=(flat, flat, flat),
        in_specs=[pl.BlockSpec(memory_space=pltpu.SMEM)] + [vm] * 4,
        out_specs=(vm, vm, vm),
        cost_estimate=pl.CostEstimate(flops=0, bytes_accessed=2_000_000, transcendentals=0),
    )(at, *pieces)


def contract(left_ref, flip_ref, val_ref, own_ref, oth_ref, out_ref, p_ref, q_ref):
    left = left_ref[...]
    flipped = flip_ref[...]
    rows = left.shape[0]
    wrapped = jnp.concatenate([left, left[:, : 3 * BLK]], 1)
    wrapped_flip = jnp.concatenate([flipped, flipped[:, : 3 * BLK]], 1)
    for b in range(NB):
        lo, hi = b * BLK, (b + 1) * BLK
        far = wrapped[:, hi : hi + 3 * BLK]
        far_flip = wrapped_flip[:, hi : hi + 3 * BLK]
        own = own_ref[lo:hi, :]
        oth = oth_ref[lo:hi, :]
        p_back = nt(far_flip, own[:, BLK : 4 * BLK])
        q_back = -nt(far, oth[:, BLK : 4 * BLK])
        if b == 0:
            p_ref[...] = jnp.zeros_like(p_ref)
            q_ref[...] = jnp.zeros_like(q_ref)
        p_ref[:, lo:hi] += p_back
        q_ref[:, lo:hi] += q_back
        p_fore = nn(left[:, lo:hi], own)
        q_fore = nn(flipped[:, lo:hi], oth)
        first = min(SENT, NB - b)
        p_ref[:, lo : lo + first * BLK] += p_fore[:, : first * BLK]
        q_ref[:, lo : lo + first * BLK] += q_fore[:, : first * BLK]
        if first < SENT:
            p_ref[:, : (SENT - first) * BLK] += p_fore[:, first * BLK :]
            q_ref[:, : (SENT - first) * BLK] += q_fore[:, first * BLK :]
    p = p_ref[...].reshape(KQ, 2, PAIR, NG)
    q = q_ref[...].reshape(KQ, 2, PAIR, NG)
    half = rows // 2
    x_real = (p[:, 0] + q[:, 1]).reshape(half, NG).astype(BF)
    x_imag = (q[:, 0] - p[:, 1]).reshape(half, NG).astype(BF)
    val = val_ref[...]
    g1 = nt(x_real, val)
    g2 = nt(x_imag, val)
    r = lax.broadcasted_iota(jnp.int32, (half, rows), 0)
    c = lax.broadcasted_iota(jnp.int32, (half, rows), 1)
    same = r // PAIR == c // (2 * PAIR)
    g1 = jnp.where(same, g1, 0.0)
    g2 = jnp.where(same, g2, 0.0)
    c = lax.broadcasted_iota(jnp.int32, (rows, 128), 0)
    l = lax.broadcasted_iota(jnp.int32, (rows, 128), 1)
    hit = c % PAIR == l % PAIR
    part = (c // PAIR) % 2
    want = l // 64
    e1 = jnp.where(hit & (part == want), 1.0, 0.0)
    e2 = jnp.where(hit & (part != want), jnp.where(want == 0, -1.0, 1.0), 0.0)
    t = nn(g1, e1, lax.Precision.HIGHEST) + nn(g2, e2, lax.Precision.HIGHEST)
    r = lax.broadcasted_iota(jnp.int32, (half, 128), 0)
    l = lax.broadcasted_iota(jnp.int32, (half, 128), 1)
    t = jnp.where(r % 4 == (l // PAIR) % 4, t, 0.0)
    o = lax.broadcasted_iota(jnp.int32, (4 * 8, half), 0)
    r = lax.broadcasted_iota(jnp.int32, (4 * 8, half), 1)
    e3 = jnp.where((r // PAIR == o % 8) & ((r % PAIR) // 4 == o // 8), 1.0, 0.0)
    block = nn(e3, t, lax.Precision.HIGHEST)
    for slot in range(16):
        g = slot % 4
        out_ref[slot, :, :] = block[g * 8 : g * 8 + KQ, :]


def contracted(left, flipped, val, own, oth):
    vm = pl.BlockSpec(memory_space=pltpu.VMEM)
    return pl.pallas_call(
        contract,
        out_shape=jax.ShapeDtypeStruct((16, KQ, 128), F32),
        in_specs=[vm] * 5,
        out_specs=vm,
        scratch_shapes=[
            pltpu.VMEM((2 * KQ * PAIR, NG), F32),
            pltpu.VMEM((2 * KQ * PAIR, NG), F32),
        ],
        cost_estimate=pl.CostEstimate(
            flops=1_600_000_000, bytes_accessed=4_000_000, transcendentals=0
        ),
    )(left, flipped, val, own, oth)


def pick_rows(at_ref, came_ref, fwd_ref, pay_ref, got_ref, sem):
    copy = pltpu.make_async_copy(came_ref, got_ref, sem)
    copy.start()
    copy.wait()
    xl = at_ref[0]
    yl = at_ref[1]
    for q in range(Q):
        base = (q // 2) * 8 + (q % 2) * 2
        other = at_ref[2 + q]
        begin = at_ref[6 + q]
        for t in range(KQ):
            row = got_ref[base + yl * 4 + t // 3, pl.ds(xl * 3 + t % 3, 1), :]
            fwd_ref[q, pl.ds(t, 1), 0, :] = row[:, :64]
            fwd_ref[q, pl.ds(t, 1), 1, :] = row[:, 64:]
            col = lax.rem(begin + t, 12)
            slot = base + (col // 6) * 4 + (col % 6) // 3
            pay_ref[0, pl.ds(q * KQ + t, 1), :] = got_ref[slot, pl.ds(other * 3 + col % 3, 1), :]
    pay = pay_ref[0]
    for slot in range(1, 32):
        pay_ref[slot, :, :] = pay


def pick_back(at_ref, came_ref, out_ref, got_ref, sem):
    copies = [
        pltpu.make_async_copy(came_ref.at[at_ref[q]], got_ref.at[q], sem.at[q]) for q in range(Q)
    ]
    for copy in copies:
        copy.start()
    for q in range(Q):
        copies[q].wait()
        rows = got_ref[q, q * KQ : (q + 1) * KQ, :]
        out_ref[q, :, 0, :] = rows[:, :64]
        out_ref[q, :, 1, :] = rows[:, 64:]


def local(cond, val, screened, k_plus):
    xl, yl, core = lax.axis_index("xl"), lax.axis_index("yl"), lax.axis_index("c")
    z, yh = lax.axis_index("z"), lax.axis_index("yh")
    w = lax.all_to_all(screened.reshape(8, 8, 256), ("xl", "xh", "c"), 0, 0)
    w = jnp.transpose(w.reshape(2, 4, 8, 256), (0, 2, 1, 3)).reshape(2, 8, NG)
    w = jnp.concatenate([w, w[:, :, : 4 * BLK]], 2)
    cut = [
        lax.dynamic_slice_in_dim(w[i], (4 * i + z // 2) * BLK, SENT * BLK, 1) for i in range(2)
    ]
    w = jnp.stack(cut, 0)
    w = jnp.broadcast_to(w, (64,) + w.shape)
    w = lax.all_to_all(w, ("z", "yh", "yl"), 0, 0)
    own = jnp.transpose(w, (1, 0, 2, 3)).reshape(NG, SENT * BLK)
    oth = lax.ppermute(own, "c", [(0, 1), (1, 0)])

    x = xl * 2 + lax.axis_index("xh")

    slots = [pairs.reshape(4, 2, 3, 2, PAIR, 256) for pairs in (cond, val)]
    keep = [lax.dynamic_index_in_dim(part, core, 1, False) for part in slots]
    given = [lax.dynamic_index_in_dim(part, 1 - core, 1, False) for part in slots]
    given = jnp.stack(given, 0)
    given = lax.ppermute(given, "c", [(0, 1), (1, 0)])
    pieces = []
    for s in range(4):
        both = [
            lax.dynamic_index_in_dim(part, x ^ s, 0, False)
            for part in (keep[0], given[0], keep[1], given[1])
        ]
        piece = jnp.stack(both, 0).reshape(2, 2, 3, 2, PAIR, 256)
        if s:
            piece = lax.ppermute(piece, ("xl", "xh"), [(i, i ^ s) for i in range(4)])
        pieces.append(piece)
    here_x = jnp.stack([x, core]).astype(jnp.int32)
    left, flipped, right = assembled(here_x, pieces)
    slots = contracted(left, flipped, right, own, oth)
    got = lax.all_to_all(slots, ("xl", "yl", "xh", "c"), 0, 0)
    corner = k_plus[:, 0]
    row_step, col_step = corner // 12, corner % 12
    here = z * 4 + yh
    other = xl ^ ((here + row_step) // 32 % 2)
    begin = (6 * yl - col_step + 12) % 12
    at = jnp.concatenate([jnp.stack([xl, yl]), other, begin]).astype(jnp.int32)
    vm = pl.BlockSpec(memory_space=pltpu.VMEM)
    sm = pl.BlockSpec(memory_space=pltpu.SMEM)
    anywhere = pl.BlockSpec(memory_space=pl.ANY)
    out = jax.ShapeDtypeStruct((Q, KQ, 2, 64), F32)
    forward, pay = pl.pallas_call(
        pick_rows,
        out_shape=(out, jax.ShapeDtypeStruct((32, Q * KQ, 128), F32)),
        in_specs=[sm, anywhere],
        out_specs=(vm, vm),
        scratch_shapes=[pltpu.VMEM((16, KQ, 128), F32), pltpu.SemaphoreType.DMA],
        compiler_params=pltpu.CompilerParams(vmem_limit_bytes=8 << 20),
    )(at, got)
    came = lax.all_to_all(pay, ("z", "yh"), 0, 0)
    source = ((here - row_step) % 32).astype(jnp.int32)
    back = pl.pallas_call(
        pick_back,
        out_shape=out,
        in_specs=[sm, anywhere],
        out_specs=vm,
        scratch_shapes=[pltpu.VMEM((Q, Q * KQ, 128), F32), pltpu.SemaphoreType.DMA((Q,))],
        compiler_params=pltpu.CompilerParams(vmem_limit_bytes=8 << 20),
    )(source, came)
    return forward, back


def solution(mesh):
    fine = Mesh(mesh.devices.reshape(2, 8, 4, 2, 2, 2), ("xl", "z", "yh", "yl", "xh", "c"))
    ka, ga = ("xl", "z", "yh", "yl"), ("xh", "c")
    in_specs = (
        P(None, ka, None, None, ga),
        P(None, ka, None, None, ga),
        P(None, None, ka, ga),
        P(),
    )
    out_specs = (P(None, ka, None, ga), P(None, ka, None, ga))
    return jax.shard_map(local, mesh=fine, in_specs=in_specs, out_specs=out_specs, check_vma=False)
```

```python
import jax
import jax.numpy as jnp
from jax import lax
from jax.experimental import pallas as pl
from jax.experimental.pallas import tpu as pltpu
from jax.sharding import Mesh
from jax.sharding import PartitionSpec as P

NG = 1024
Q = 4
PAIR = 16
BLK = 128
NB = NG // BLK
SENT = 5
KQ = 6
BF = jnp.bfloat16
F32 = jnp.float32


def nt(left, right, precision=None):
    return lax.dot_general(
        left, right, (((1,), (1,)), ((), ())), preferred_element_type=F32, precision=precision
    )


def nn(left, right, precision=None):
    return jnp.dot(left, right, preferred_element_type=F32, precision=precision)


def assemble(at_ref, *refs):
    pieces, (left_ref, flip_ref, val_ref) = refs[:4], refs[4:]
    x, core = at_ref[0], at_ref[1]
    minus = jnp.where(core == 0, 1.0, -1.0).astype(BF)
    for s in range(4):
        xl = (x ^ s) // 2
        for t in range(2):
            g = ((x ^ s) % 2) * 2 + (core ^ t)
            lanes = pl.ds(pl.multiple_of(g * 256, 256), 256)
            for j in range(3):
                row = xl * 96 + j * 32
                whole = pl.ds(pl.multiple_of(row, 32), 32)
                val_ref[whole, lanes] = pieces[s][1, t, j].reshape(32, 256)
                for r in range(2):
                    part = pl.ds(pl.multiple_of(row + (r ^ core) * PAIR, PAIR), PAIR)
                    piece = pieces[s][0, t, j, r]
                    if r == 0:
                        piece = piece * minus
                    left_ref[part, lanes] = piece
                    flip_ref[part, lanes] = piece * minus


def assembled(at, pieces):
    vm = pl.BlockSpec(memory_space=pltpu.VMEM)
    flat = jax.ShapeDtypeStruct((2 * KQ * PAIR, NG), BF)
    return pl.pallas_call(
        assemble,
        out_shape=(flat, flat, flat),
        in_specs=[pl.BlockSpec(memory_space=pltpu.SMEM)] + [vm] * 4,
        out_specs=(vm, vm, vm),
        cost_estimate=pl.CostEstimate(flops=0, bytes_accessed=2_000_000, transcendentals=0),
    )(at, *pieces)


def contract(left_in, flip_in, val_in, own_in, oth_in, out_ref, *scratch):
    left_ref, flip_ref, val_ref, own_ref, oth_ref, p_ref, q_ref, sem, own_sem, oth_sem = scratch
    first = [
        pltpu.make_async_copy(left_in, left_ref, sem.at[0]),
        pltpu.make_async_copy(flip_in, flip_ref, sem.at[1]),
    ]
    last = pltpu.make_async_copy(val_in, val_ref, sem.at[2])

    def chunks(source, target, sems):
        return [
            pltpu.make_async_copy(
                source.at[pl.ds(i * BLK, BLK), :], target.at[pl.ds(i * BLK, BLK), :], sems.at[i]
            )
            for i in range(4)
        ]

    own_copies = chunks(own_in, own_ref, own_sem)
    oth_copies = chunks(oth_in, oth_ref, oth_sem)
    for copy in first + own_copies + oth_copies + [last]:
        copy.start()
    for copy in first:
        copy.wait()
    left = left_ref[...]
    flipped = flip_ref[...]
    rows = left.shape[0]

    def screen(ahead, behind, w_ref, sum_ref, copies, negate):
        sum_ref[...] = jnp.zeros_like(sum_ref)
        wrapped = jnp.concatenate([behind, behind[:, : 3 * BLK]], 1)
        for i in range(4):
            copies[i].wait()
            for half in range(2):
                b = i + 4 * half
                lo, hi = b * BLK, (b + 1) * BLK
                sent = SENT - half
                w = w_ref[i * BLK : (i + 1) * BLK, half * SENT * BLK : (half + 1) * SENT * BLK - half * BLK]
                back = nt(wrapped[:, hi : hi + (sent - 1) * BLK], w[:, BLK:])
                sum_ref[:, lo:hi] += -back if negate else back
                fore = nn(ahead[:, lo:hi], w)
                direct = min(sent, NB - b)
                sum_ref[:, lo : lo + direct * BLK] += fore[:, : direct * BLK]
                if direct < sent:
                    sum_ref[:, : (sent - direct) * BLK] += fore[:, direct * BLK :]

    screen(left, flipped, own_ref, p_ref, own_copies, False)
    screen(flipped, left, oth_ref, q_ref, oth_copies, True)
    last.wait()
    p = p_ref[...].reshape(KQ, 2, PAIR, NG)
    q = q_ref[...].reshape(KQ, 2, PAIR, NG)
    half = rows // 2
    x_real = (p[:, 0] + q[:, 1]).reshape(half, NG).astype(BF)
    x_imag = (q[:, 0] - p[:, 1]).reshape(half, NG).astype(BF)
    val = val_ref[...]
    g1 = nt(x_real, val)
    g2 = nt(x_imag, val)
    r = lax.broadcasted_iota(jnp.int32, (half, rows), 0)
    c = lax.broadcasted_iota(jnp.int32, (half, rows), 1)
    same = r // PAIR == c // (2 * PAIR)
    g1 = jnp.where(same, g1, 0.0)
    g2 = jnp.where(same, g2, 0.0)
    c = lax.broadcasted_iota(jnp.int32, (rows, 128), 0)
    l = lax.broadcasted_iota(jnp.int32, (rows, 128), 1)
    hit = c % PAIR == l % PAIR
    part = (c // PAIR) % 2
    want = l // 64
    e1 = jnp.where(hit & (part == want), 1.0, 0.0)
    e2 = jnp.where(hit & (part != want), jnp.where(want == 0, -1.0, 1.0), 0.0)
    t = nn(g1, e1, lax.Precision.HIGHEST) + nn(g2, e2, lax.Precision.HIGHEST)
    r = lax.broadcasted_iota(jnp.int32, (half, 128), 0)
    l = lax.broadcasted_iota(jnp.int32, (half, 128), 1)
    t = jnp.where(r % 4 == (l // PAIR) % 4, t, 0.0)
    o = lax.broadcasted_iota(jnp.int32, (4 * 8, half), 0)
    r = lax.broadcasted_iota(jnp.int32, (4 * 8, half), 1)
    e3 = jnp.where((r // PAIR == o % 8) & ((r % PAIR) // 4 == o // 8), 1.0, 0.0)
    block = nn(e3, t, lax.Precision.HIGHEST)
    for slot in range(16):
        g = slot % 4
        out_ref[slot, :, :] = block[g * 8 : g * 8 + KQ, :]


def contracted(left, flipped, val, own, oth):
    sums = (2 * KQ * PAIR, NG)
    sent = (NG // 2, (2 * SENT - 1) * BLK)
    return pl.pallas_call(
        contract,
        out_shape=jax.ShapeDtypeStruct((16, KQ, 128), F32),
        in_specs=[pl.BlockSpec(memory_space=pl.ANY)] * 5,
        out_specs=pl.BlockSpec(memory_space=pltpu.VMEM),
        scratch_shapes=[pltpu.VMEM(sums, BF)] * 3
        + [pltpu.VMEM(sent, BF)] * 2
        + [pltpu.VMEM(sums, F32)] * 2
        + [pltpu.SemaphoreType.DMA((3,)), pltpu.SemaphoreType.DMA((4,)), pltpu.SemaphoreType.DMA((4,))],
        compiler_params=pltpu.CompilerParams(vmem_limit_bytes=32 << 20),
        cost_estimate=pl.CostEstimate(
            flops=1_600_000_000, bytes_accessed=4_000_000, transcendentals=0
        ),
    )(left, flipped, val, own, oth)


def pick_rows(at_ref, came_ref, fwd_ref, pay_ref, got_ref, sem):
    copy = pltpu.make_async_copy(came_ref, got_ref, sem)
    copy.start()
    copy.wait()
    xl = at_ref[0]
    yl = at_ref[1]
    for q in range(Q):
        base = (q // 2) * 8 + (q % 2) * 2
        other = at_ref[2 + q]
        begin = at_ref[6 + q]
        for t in range(KQ):
            row = got_ref[base + yl * 4 + t // 3, pl.ds(xl * 3 + t % 3, 1), :]
            fwd_ref[q, pl.ds(t, 1), 0, :] = row[:, :64]
            fwd_ref[q, pl.ds(t, 1), 1, :] = row[:, 64:]
            col = lax.rem(begin + t, 12)
            slot = base + (col // 6) * 4 + (col % 6) // 3
            pay_ref[0, pl.ds(q * KQ + t, 1), :] = got_ref[slot, pl.ds(other * 3 + col % 3, 1), :]
    pay = pay_ref[0]
    for slot in range(1, 32):
        pay_ref[slot, :, :] = pay


def pick_back(at_ref, came_ref, out_ref, got_ref, sem):
    copies = [
        pltpu.make_async_copy(came_ref.at[at_ref[q]], got_ref.at[q], sem.at[q]) for q in range(Q)
    ]
    for copy in copies:
        copy.start()
    for q in range(Q):
        copies[q].wait()
        rows = got_ref[q, q * KQ : (q + 1) * KQ, :]
        out_ref[q, :, 0, :] = rows[:, :64]
        out_ref[q, :, 1, :] = rows[:, 64:]


def local(cond, val, screened, k_plus):
    xl, yl, core = lax.axis_index("xl"), lax.axis_index("yl"), lax.axis_index("c")
    z, yh = lax.axis_index("z"), lax.axis_index("yh")
    w = lax.all_to_all(screened.reshape(8, 8, 256), ("xl", "xh", "c"), 0, 0)
    w = jnp.transpose(w.reshape(2, 4, 8, 256), (0, 2, 1, 3)).reshape(2, 8, NG)
    w = jnp.concatenate([w, w[:, :, : 4 * BLK]], 2)
    cut = [
        lax.dynamic_slice_in_dim(w[i], (4 * i + z // 2) * BLK, (SENT - i) * BLK, 1)
        for i in range(2)
    ]
    w = jnp.concatenate(cut, 1)
    w = jnp.broadcast_to(w, (64,) + w.shape)
    w = lax.all_to_all(w, ("z", "yh", "yl"), 0, 0)
    own = w.reshape(NG // 2, (2 * SENT - 1) * BLK)
    oth = lax.ppermute(own, "c", [(0, 1), (1, 0)])

    x = xl * 2 + lax.axis_index("xh")

    slots = [pairs.reshape(4, 2, 3, 2, PAIR, 256) for pairs in (cond, val)]
    keep = [lax.dynamic_index_in_dim(part, core, 1, False) for part in slots]
    given = [lax.dynamic_index_in_dim(part, 1 - core, 1, False) for part in slots]
    given = jnp.stack(given, 0)
    given = lax.ppermute(given, "c", [(0, 1), (1, 0)])
    pieces = []
    for s in range(4):
        both = [
            lax.dynamic_index_in_dim(part, x ^ s, 0, False)
            for part in (keep[0], given[0], keep[1], given[1])
        ]
        piece = jnp.stack(both, 0).reshape(2, 2, 3, 2, PAIR, 256)
        if s:
            piece = lax.ppermute(piece, ("xl", "xh"), [(i, i ^ s) for i in range(4)])
        pieces.append(piece)
    here_x = jnp.stack([x, core]).astype(jnp.int32)
    left, flipped, right = assembled(here_x, pieces)
    slots = contracted(left, flipped, right, own, oth)
    got = lax.all_to_all(slots, ("xl", "yl", "xh", "c"), 0, 0)
    corner = k_plus[:, 0]
    row_step, col_step = corner // 12, corner % 12
    here = z * 4 + yh
    other = xl ^ ((here + row_step) // 32 % 2)
    begin = (6 * yl - col_step + 12) % 12
    at = jnp.concatenate([jnp.stack([xl, yl]), other, begin]).astype(jnp.int32)
    vm = pl.BlockSpec(memory_space=pltpu.VMEM)
    sm = pl.BlockSpec(memory_space=pltpu.SMEM)
    anywhere = pl.BlockSpec(memory_space=pl.ANY)
    out = jax.ShapeDtypeStruct((Q, KQ, 2, 64), F32)
    forward, pay = pl.pallas_call(
        pick_rows,
        out_shape=(out, jax.ShapeDtypeStruct((32, Q * KQ, 128), F32)),
        in_specs=[sm, anywhere],
        out_specs=(vm, vm),
        scratch_shapes=[pltpu.VMEM((16, KQ, 128), F32), pltpu.SemaphoreType.DMA],
        compiler_params=pltpu.CompilerParams(vmem_limit_bytes=8 << 20),
    )(at, got)
    came = lax.all_to_all(pay, ("z", "yh"), 0, 0)
    source = ((here - row_step) % 32).astype(jnp.int32)
    back = pl.pallas_call(
        pick_back,
        out_shape=out,
        in_specs=[sm, anywhere],
        out_specs=vm,
        scratch_shapes=[pltpu.VMEM((Q, Q * KQ, 128), F32), pltpu.SemaphoreType.DMA((Q,))],
        compiler_params=pltpu.CompilerParams(vmem_limit_bytes=8 << 20),
    )(source, came)
    return forward, back


def solution(mesh):
    fine = Mesh(mesh.devices.reshape(2, 8, 4, 2, 2, 2), ("xl", "z", "yh", "yl", "xh", "c"))
    ka, ga = ("xl", "z", "yh", "yl"), ("xh", "c")
    in_specs = (
        P(None, ka, None, None, ga),
        P(None, ka, None, None, ga),
        P(None, None, ka, ga),
        P(),
    )
    out_specs = (P(None, ka, None, ga), P(None, ka, None, ga))
    return jax.shard_map(local, mesh=fine, in_specs=in_specs, out_specs=out_specs, check_vma=False)
```

```python
import jax
import jax.numpy as jnp
from jax import lax
from jax.experimental import pallas as pl
from jax.experimental.pallas import tpu as pltpu
from jax.sharding import Mesh
from jax.sharding import PartitionSpec as P

NG = 1024
Q = 4
PAIR = 16
BLK = 128
NB = NG // BLK
SENT = 5
KQ = 6
BF = jnp.bfloat16
F32 = jnp.float32


def nt(left, right, precision=None):
    return lax.dot_general(
        left, right, (((1,), (1,)), ((), ())), preferred_element_type=F32, precision=precision
    )


def nn(left, right, precision=None):
    return jnp.dot(left, right, preferred_element_type=F32, precision=precision)


def assemble(at_ref, *refs):
    pieces, (left_ref, flip_ref, val_ref) = refs[:4], refs[4:]
    x, core = at_ref[0], at_ref[1]
    minus = jnp.where(core == 0, 1.0, -1.0).astype(BF)
    for s in range(4):
        xl = (x ^ s) // 2
        for t in range(2):
            g = ((x ^ s) % 2) * 2 + (core ^ t)
            lanes = pl.ds(pl.multiple_of(g * 256, 256), 256)
            for j in range(3):
                row = xl * 96 + j * 32
                whole = pl.ds(pl.multiple_of(row, 32), 32)
                val_ref[whole, lanes] = pieces[s][1, t, j].reshape(32, 256)
                for r in range(2):
                    part = pl.ds(pl.multiple_of(row + (r ^ core) * PAIR, PAIR), PAIR)
                    piece = pieces[s][0, t, j, r]
                    if r == 0:
                        piece = piece * minus
                    left_ref[part, lanes] = piece
                    flip_ref[part, lanes] = piece * minus


def assembled(at, pieces):
    vm = pl.BlockSpec(memory_space=pltpu.VMEM)
    flat = jax.ShapeDtypeStruct((2 * KQ * PAIR, NG), BF)
    return pl.pallas_call(
        assemble,
        out_shape=(flat, flat, flat),
        in_specs=[pl.BlockSpec(memory_space=pltpu.SMEM)] + [vm] * 4,
        out_specs=(vm, vm, vm),
        compiler_params=pltpu.CompilerParams(vmem_limit_bytes=16 << 20),
        cost_estimate=pl.CostEstimate(flops=0, bytes_accessed=2_000_000, transcendentals=0),
    )(at, *pieces)


def stacked(w_ref, j):
    zero = jnp.zeros((BLK, BLK), BF)

    def block(b, d):
        half, i = b // 4, b % 4
        if d < 0 or d > 4 - half:
            return zero
        lane = half * SENT * BLK + d * BLK
        return w_ref[i * BLK : (i + 1) * BLK, lane : lane + BLK]

    first = j - 4 if j >= 4 else j - 3
    direct = jnp.concatenate(
        [
            jnp.concatenate([block(b % NB, j - b), block(b % NB, j + 1 - b)], 1)
            for b in range(first, j + 2)
        ],
        0,
    )
    width = 4 if j >= 4 else 5
    mirrored = jnp.concatenate(
        [
            jnp.concatenate([block(row, j + 1 + m - row) if j + 1 + m > row else zero for m in range(width)], 1)
            for row in (j, j + 1)
        ],
        0,
    )
    return first, direct, width, mirrored


def contract(left_ref, flip_ref, val_ref, own_ref, oth_ref, out_ref):
    rows = left_ref.shape[0]
    half = rows // 2

    def wrapped(ref):
        x = ref[...]
        return jnp.concatenate([x[:, 5 * BLK :], x, x[:, : 3 * BLK]], 1)

    left, flipped = wrapped(left_ref), wrapped(flip_ref)

    def lanes(x, begin, count):
        return x[:, (begin + 3) * BLK : (begin + 3 + count) * BLK]

    g1 = jnp.zeros((half, rows), F32)
    g2 = jnp.zeros((half, rows), F32)
    for j in range(0, NB, 2):
        sums = []
        for ref, ahead, behind in ((own_ref, left, flipped), (oth_ref, flipped, left)):
            first, direct, width, mirrored = stacked(ref, j)
            fore = nn(lanes(ahead, first, j + 2 - first), direct)
            back = nt(lanes(behind, j + 1, width), mirrored)
            sums.append((fore + back if ref is own_ref else fore - back).reshape(KQ, 2, PAIR, 2 * BLK))
        p, q = sums
        x_real = (p[:, 0] + q[:, 1]).reshape(half, 2 * BLK).astype(BF)
        x_imag = (q[:, 0] - p[:, 1]).reshape(half, 2 * BLK).astype(BF)
        val = val_ref[:, j * BLK : (j + 2) * BLK]
        g1 += nt(x_real, val)
        g2 += nt(x_imag, val)
    r = lax.broadcasted_iota(jnp.int32, (half, rows), 0)
    c = lax.broadcasted_iota(jnp.int32, (half, rows), 1)
    same = r // PAIR == c // (2 * PAIR)
    g1 = jnp.where(same, g1, 0.0)
    g2 = jnp.where(same, g2, 0.0)
    c = lax.broadcasted_iota(jnp.int32, (rows, 128), 0)
    l = lax.broadcasted_iota(jnp.int32, (rows, 128), 1)
    hit = c % PAIR == l % PAIR
    part = (c // PAIR) % 2
    want = l // 64
    e1 = jnp.where(hit & (part == want), 1.0, 0.0)
    e2 = jnp.where(hit & (part != want), jnp.where(want == 0, -1.0, 1.0), 0.0)
    t = nn(g1, e1, lax.Precision.HIGHEST) + nn(g2, e2, lax.Precision.HIGHEST)
    r = lax.broadcasted_iota(jnp.int32, (half, 128), 0)
    l = lax.broadcasted_iota(jnp.int32, (half, 128), 1)
    t = jnp.where(r % 4 == (l // PAIR) % 4, t, 0.0)
    o = lax.broadcasted_iota(jnp.int32, (4 * 8, half), 0)
    r = lax.broadcasted_iota(jnp.int32, (4 * 8, half), 1)
    e3 = jnp.where((r // PAIR == o % 8) & ((r % PAIR) // 4 == o // 8), 1.0, 0.0)
    block = nn(e3, t, lax.Precision.HIGHEST)
    for slot in range(16):
        g = slot % 4
        out_ref[slot, :, :] = block[g * 8 : g * 8 + KQ, :]


def contracted(left, flipped, val, own, oth):
    return pl.pallas_call(
        contract,
        out_shape=jax.ShapeDtypeStruct((16, KQ, 128), F32),
        in_specs=[pl.BlockSpec(memory_space=pltpu.VMEM)] * 5,
        out_specs=pl.BlockSpec(memory_space=pltpu.VMEM),
        compiler_params=pltpu.CompilerParams(vmem_limit_bytes=32 << 20),
        cost_estimate=pl.CostEstimate(
            flops=1_600_000_000, bytes_accessed=4_000_000, transcendentals=0
        ),
    )(left, flipped, val, own, oth)


def pick_rows(at_ref, got_ref, fwd_ref, pay_ref):
    xl = at_ref[0]
    yl = at_ref[1]
    for q in range(Q):
        base = (q // 2) * 8 + (q % 2) * 2
        other = at_ref[2 + q]
        begin = at_ref[6 + q]
        for t in range(KQ):
            row = got_ref[base + yl * 4 + t // 3, pl.ds(xl * 3 + t % 3, 1), :]
            fwd_ref[q, pl.ds(t, 1), 0, :] = row[:, :64]
            fwd_ref[q, pl.ds(t, 1), 1, :] = row[:, 64:]
            col = lax.rem(begin + t, 12)
            slot = base + (col // 6) * 4 + (col % 6) // 3
            pay_ref[0, pl.ds(q * KQ + t, 1), :] = got_ref[slot, pl.ds(other * 3 + col % 3, 1), :]
    pay = pay_ref[0]
    for slot in range(1, 32):
        pay_ref[slot, :, :] = pay


def pick_back(at_ref, came_ref, out_ref):
    for q in range(Q):
        rows = came_ref[at_ref[q], q * KQ : (q + 1) * KQ, :]
        out_ref[q, :, 0, :] = rows[:, :64]
        out_ref[q, :, 1, :] = rows[:, 64:]


def local(cond, val, screened, k_plus):
    xl, yl, core = lax.axis_index("xl"), lax.axis_index("yl"), lax.axis_index("c")
    z, yh = lax.axis_index("z"), lax.axis_index("yh")
    w = lax.all_to_all(screened.reshape(8, 8, 256), ("xl", "xh", "c"), 0, 0)
    w = jnp.transpose(w.reshape(2, 4, 8, 256), (0, 2, 1, 3)).reshape(2, 8, NG)
    w = jnp.concatenate([w, w[:, :, : 4 * BLK]], 2)
    cut = [
        lax.dynamic_slice_in_dim(w[i], (4 * i + z // 2) * BLK, (SENT - i) * BLK, 1)
        for i in range(2)
    ]
    w = jnp.concatenate(cut, 1)
    w = jnp.broadcast_to(w, (64,) + w.shape)
    w = lax.all_to_all(w, ("z", "yh", "yl"), 0, 0)
    own = w.reshape(NG // 2, (2 * SENT - 1) * BLK)
    oth = lax.ppermute(own, "c", [(0, 1), (1, 0)])

    x = xl * 2 + lax.axis_index("xh")

    slots = [pairs.reshape(4, 2, 3, 2, PAIR, 256) for pairs in (cond, val)]
    keep = [lax.dynamic_index_in_dim(part, core, 1, False) for part in slots]
    given = [lax.dynamic_index_in_dim(part, 1 - core, 1, False) for part in slots]
    given = jnp.stack(given, 0)
    given = lax.ppermute(given, "c", [(0, 1), (1, 0)])
    pieces = []
    for s in range(4):
        both = [
            lax.dynamic_index_in_dim(part, x ^ s, 0, False)
            for part in (keep[0], given[0], keep[1], given[1])
        ]
        piece = jnp.stack(both, 0).reshape(2, 2, 3, 2, PAIR, 256)
        if s:
            piece = lax.ppermute(piece, ("xl", "xh"), [(i, i ^ s) for i in range(4)])
        pieces.append(piece)
    here_x = jnp.stack([x, core]).astype(jnp.int32)
    left, flipped, right = assembled(here_x, pieces)
    slots = contracted(left, flipped, right, own, oth)
    got = lax.all_to_all(slots, ("xl", "yl", "xh", "c"), 0, 0)
    corner = k_plus[:, 0]
    row_step, col_step = corner // 12, corner % 12
    here = z * 4 + yh
    other = xl ^ ((here + row_step) // 32 % 2)
    begin = (6 * yl - col_step + 12) % 12
    at = jnp.concatenate([jnp.stack([xl, yl]), other, begin]).astype(jnp.int32)
    vm = pl.BlockSpec(memory_space=pltpu.VMEM)
    sm = pl.BlockSpec(memory_space=pltpu.SMEM)
    out = jax.ShapeDtypeStruct((Q, KQ, 2, 64), F32)
    forward, pay = pl.pallas_call(
        pick_rows,
        out_shape=(out, jax.ShapeDtypeStruct((32, Q * KQ, 128), F32)),
        in_specs=[sm, vm],
        out_specs=(vm, vm),
        compiler_params=pltpu.CompilerParams(vmem_limit_bytes=8 << 20),
    )(at, got)
    came = lax.all_to_all(pay, ("z", "yh"), 0, 0)
    source = ((here - row_step) % 32).astype(jnp.int32)
    back = pl.pallas_call(
        pick_back,
        out_shape=out,
        in_specs=[sm, vm],
        out_specs=vm,
        compiler_params=pltpu.CompilerParams(vmem_limit_bytes=8 << 20),
    )(source, came)
    return forward, back


def solution(mesh):
    fine = Mesh(mesh.devices.reshape(2, 8, 4, 2, 2, 2), ("xl", "z", "yh", "yl", "xh", "c"))
    ka, ga = ("xl", "z", "yh", "yl"), ("xh", "c")
    in_specs = (
        P(None, ka, None, None, ga),
        P(None, ka, None, None, ga),
        P(None, None, ka, ga),
        P(),
    )
    out_specs = (P(None, ka, None, ga), P(None, ka, None, ga))
    return jax.shard_map(local, mesh=fine, in_specs=in_specs, out_specs=out_specs, check_vma=False)
```

```python
import jax
import jax.numpy as jnp
from jax import lax
from jax.experimental import pallas as pl
from jax.experimental.pallas import tpu as pltpu
from jax.sharding import Mesh
from jax.sharding import PartitionSpec as P

NG = 1024
Q = 4
PAIR = 16
BLK = 128
NB = NG // BLK
SENT = 5
KQ = 6
BF = jnp.bfloat16
F32 = jnp.float32


def nt(left, right, precision=None):
    return lax.dot_general(
        left, right, (((1,), (1,)), ((), ())), preferred_element_type=F32, precision=precision
    )


def nn(left, right, precision=None):
    return jnp.dot(left, right, preferred_element_type=F32, precision=precision)


def fan(at_ref, w_ref, out_ref):
    lane = 0
    for xl in range(2):
        for d in range(SENT - xl):
            block = lax.rem(at_ref[0] + (4 * xl + d), NB)
            lanes = pl.ds(pl.multiple_of((block % 2) * BLK, BLK), BLK)
            out_ref[0, :, lane : lane + BLK] = w_ref[4 * xl + block // 2, :, lanes]
            lane += BLK
    piece = out_ref[0]
    for slot in range(1, 64):
        out_ref[slot, :, :] = piece


def fanned(at, w):
    vm = pl.BlockSpec(memory_space=pltpu.VMEM)
    return pl.pallas_call(
        fan,
        out_shape=jax.ShapeDtypeStruct((64, 8, (2 * SENT - 1) * BLK), BF),
        in_specs=[pl.BlockSpec(memory_space=pltpu.SMEM), vm],
        out_specs=vm,
        compiler_params=pltpu.CompilerParams(vmem_limit_bytes=16 << 20),
    )(at, w)


def assemble(at_ref, *refs):
    pieces, (left_ref, flip_ref, val_ref) = refs[:4], refs[4:]
    x, core = at_ref[0], at_ref[1]
    minus = jnp.where(core == 0, 1.0, -1.0).astype(BF)
    for s in range(4):
        xl = (x ^ s) // 2
        for t in range(2):
            g = ((x ^ s) % 2) * 2 + (core ^ t)
            lanes = pl.ds(pl.multiple_of(g * 256, 256), 256)
            for j in range(3):
                row = xl * 96 + j * 32
                whole = pl.ds(pl.multiple_of(row, 32), 32)
                val_ref[whole, lanes] = pieces[s][1, t, j].reshape(32, 256)
                for r in range(2):
                    part = pl.ds(pl.multiple_of(row + (r ^ core) * PAIR, PAIR), PAIR)
                    piece = pieces[s][0, t, j, r]
                    if r == 0:
                        piece = piece * minus
                    left_ref[part, lanes] = piece
                    flip_ref[part, lanes] = piece * minus


def assembled(at, pieces):
    vm = pl.BlockSpec(memory_space=pltpu.VMEM)
    flat = jax.ShapeDtypeStruct((2 * KQ * PAIR, NG), BF)
    return pl.pallas_call(
        assemble,
        out_shape=(flat, flat, flat),
        in_specs=[pl.BlockSpec(memory_space=pltpu.SMEM)] + [vm] * 4,
        out_specs=(vm, vm, vm),
        compiler_params=pltpu.CompilerParams(vmem_limit_bytes=16 << 20),
        cost_estimate=pl.CostEstimate(flops=0, bytes_accessed=2_000_000, transcendentals=0),
    )(at, *pieces)


def stacked(w_ref, j):
    zero = jnp.zeros((BLK, BLK), BF)

    def block(b, d):
        half, i = b // 4, b % 4
        if d < 0 or d > 4 - half:
            return zero
        lane = half * SENT * BLK + d * BLK
        return w_ref[i * BLK : (i + 1) * BLK, lane : lane + BLK]

    first = j - 4 if j >= 4 else j - 3
    direct = jnp.concatenate(
        [
            jnp.concatenate([block(b % NB, j - b), block(b % NB, j + 1 - b)], 1)
            for b in range(first, j + 2)
        ],
        0,
    )
    width = 4 if j >= 4 else 5
    mirrored = jnp.concatenate(
        [
            jnp.concatenate([block(row, j + 1 + m - row) if j + 1 + m > row else zero for m in range(width)], 1)
            for row in (j, j + 1)
        ],
        0,
    )
    return first, direct, width, mirrored


def wrapped(x):
    return jnp.concatenate([x[:, 5 * BLK :], x, x[:, : 3 * BLK]], 1)


def screened_pair(w_ref, ahead, behind, j):
    def lanes(x, begin, count):
        return x[:, (begin + 3) * BLK : (begin + 3 + count) * BLK]

    first, direct, width, mirrored = stacked(w_ref, j)
    return nn(lanes(ahead, first, j + 2 - first), direct), nt(lanes(behind, j + 1, width), mirrored)


def contract_own(left_ref, flip_ref, own_ref, p_ref):
    left, flipped = wrapped(left_ref[...]), wrapped(flip_ref[...])
    for j in range(0, NB, 2):
        fore, back = screened_pair(own_ref, left, flipped, j)
        p_ref[:, j * BLK : (j + 2) * BLK] = fore + back


def contract(left_ref, flip_ref, val_ref, p_ref, oth_ref, out_ref):
    rows = left_ref.shape[0]
    half = rows // 2
    left, flipped = wrapped(left_ref[...]), wrapped(flip_ref[...])
    g1 = jnp.zeros((half, rows), F32)
    g2 = jnp.zeros((half, rows), F32)
    for j in range(0, NB, 2):
        columns = slice(j * BLK, (j + 2) * BLK)
        fore, back = screened_pair(oth_ref, flipped, left, j)
        q = (fore - back).reshape(KQ, 2, PAIR, 2 * BLK)
        p = p_ref[:, columns].reshape(KQ, 2, PAIR, 2 * BLK)
        x_real = (p[:, 0] + q[:, 1]).reshape(half, 2 * BLK).astype(BF)
        x_imag = (q[:, 0] - p[:, 1]).reshape(half, 2 * BLK).astype(BF)
        val = val_ref[:, columns]
        g1 += nt(x_real, val)
        g2 += nt(x_imag, val)
    r = lax.broadcasted_iota(jnp.int32, (half, rows), 0)
    c = lax.broadcasted_iota(jnp.int32, (half, rows), 1)
    same = r // PAIR == c // (2 * PAIR)
    g1 = jnp.where(same, g1, 0.0)
    g2 = jnp.where(same, g2, 0.0)
    c = lax.broadcasted_iota(jnp.int32, (rows, 128), 0)
    l = lax.broadcasted_iota(jnp.int32, (rows, 128), 1)
    hit = c % PAIR == l % PAIR
    part = (c // PAIR) % 2
    want = l // 64
    e1 = jnp.where(hit & (part == want), 1.0, 0.0)
    e2 = jnp.where(hit & (part != want), jnp.where(want == 0, -1.0, 1.0), 0.0)
    t = nn(g1, e1, lax.Precision.HIGHEST) + nn(g2, e2, lax.Precision.HIGHEST)
    r = lax.broadcasted_iota(jnp.int32, (half, 128), 0)
    l = lax.broadcasted_iota(jnp.int32, (half, 128), 1)
    t = jnp.where(r % 4 == (l // PAIR) % 4, t, 0.0)
    o = lax.broadcasted_iota(jnp.int32, (4 * 8, half), 0)
    r = lax.broadcasted_iota(jnp.int32, (4 * 8, half), 1)
    e3 = jnp.where((r // PAIR == o % 8) & ((r % PAIR) // 4 == o // 8), 1.0, 0.0)
    block = nn(e3, t, lax.Precision.HIGHEST)
    for slot in range(16):
        g = slot % 4
        out_ref[slot, :, :] = block[g * 8 : g * 8 + KQ, :]


def contracted(left, flipped, val, own):
    vm = pl.BlockSpec(memory_space=pltpu.VMEM)
    kept = pltpu.CompilerParams(vmem_limit_bytes=24 << 20)
    cost = pl.CostEstimate(flops=800_000_000, bytes_accessed=2_000_000, transcendentals=0)
    oth = lax.ppermute(own, "c", [(0, 1), (1, 0)])
    p = pl.pallas_call(
        contract_own,
        out_shape=jax.ShapeDtypeStruct((2 * KQ * PAIR, NG), F32),
        in_specs=[vm] * 3,
        out_specs=vm,
        compiler_params=kept,
        cost_estimate=cost,
    )(left, flipped, own)
    return pl.pallas_call(
        contract,
        out_shape=jax.ShapeDtypeStruct((16, KQ, 128), F32),
        in_specs=[vm] * 5,
        out_specs=vm,
        compiler_params=kept,
        cost_estimate=cost,
    )(left, flipped, val, p, oth)


def pick_rows(at_ref, got_ref, fwd_ref, pay_ref, row_ref):
    xl = at_ref[2]
    yl = at_ref[3]
    for q in range(Q):
        base = (q // 2) * 8 + (q % 2) * 2
        other = at_ref[4 + q]
        begin = at_ref[8 + q]
        for t in range(KQ):
            row = got_ref[base + yl * 4 + t // 3, pl.ds(xl * 3 + t % 3, 1), :]
            fwd_ref[q, pl.ds(t, 1), 0, :] = row[:, :64]
            fwd_ref[q, pl.ds(t, 1), 1, :] = row[:, 64:]
            col = lax.rem(begin + t, 12)
            slot = base + (col // 6) * 4 + (col % 6) // 3
            row_ref[pl.ds(q * KQ + t, 1), :] = got_ref[slot, pl.ds(other * 3 + col % 3, 1), :]
    pay = row_ref[...].astype(BF)
    for slot in range(32):
        pay_ref[slot, :, :] = pay


def pick_back(at_ref, came_ref, out_ref):
    for q in range(Q):
        rows = came_ref[at_ref[12 + q]].astype(F32)[q * KQ : (q + 1) * KQ, :]
        out_ref[q, :, 0, :] = rows[:, :64]
        out_ref[q, :, 1, :] = rows[:, 64:]


def local(cond, val, screened, k_plus):
    xl, yl, core = lax.axis_index("xl"), lax.axis_index("yl"), lax.axis_index("c")
    z, yh = lax.axis_index("z"), lax.axis_index("yh")
    w = lax.all_to_all(screened.reshape(8, 8, 256), ("xl", "xh", "c"), 0, 0)
    w = fanned((z // 2).astype(jnp.int32).reshape(1), w)
    w = lax.all_to_all(w, ("z", "yh", "yl"), 0, 0)
    own = w.reshape(NG // 2, (2 * SENT - 1) * BLK)

    x = xl * 2 + lax.axis_index("xh")

    slots = [pairs.reshape(4, 2, 3, 2, PAIR, 256) for pairs in (cond, val)]
    keep = [lax.dynamic_index_in_dim(part, core, 1, False) for part in slots]
    given = [lax.dynamic_index_in_dim(part, 1 - core, 1, False) for part in slots]
    given = jnp.stack(given, 0)
    given = lax.ppermute(given, "c", [(0, 1), (1, 0)])
    pieces = []
    for s in range(4):
        both = [
            lax.dynamic_index_in_dim(part, x ^ s, 0, False)
            for part in (keep[0], given[0], keep[1], given[1])
        ]
        piece = jnp.stack(both, 0).reshape(2, 2, 3, 2, PAIR, 256)
        if s:
            piece = lax.ppermute(piece, ("xl", "xh"), [(i, i ^ s) for i in range(4)])
        pieces.append(piece)
    corner = k_plus[:, 0]
    row_step, col_step = corner // 12, corner % 12
    here = z * 4 + yh
    other = xl ^ ((here + row_step) // 32 % 2)
    begin = (6 * yl - col_step + 12) % 12
    source = (here - row_step) % 32
    at = jnp.concatenate([jnp.stack([x, core, xl, yl]), other, begin, source]).astype(jnp.int32)
    left, flipped, right = assembled(at, pieces)
    slots = contracted(left, flipped, right, own)
    got = lax.all_to_all(slots, ("xl", "yl", "xh", "c"), 0, 0)
    vm = pl.BlockSpec(memory_space=pltpu.VMEM)
    sm = pl.BlockSpec(memory_space=pltpu.SMEM)
    out = jax.ShapeDtypeStruct((Q, KQ, 2, 64), F32)
    forward, pay = pl.pallas_call(
        pick_rows,
        out_shape=(out, jax.ShapeDtypeStruct((32, Q * KQ, 128), BF)),
        in_specs=[sm, vm],
        out_specs=(vm, vm),
        scratch_shapes=[pltpu.VMEM((Q * KQ, 128), F32)],
        compiler_params=pltpu.CompilerParams(vmem_limit_bytes=8 << 20),
    )(at, got)
    came = lax.all_to_all(pay, ("z", "yh"), 0, 0)
    back = pl.pallas_call(
        pick_back,
        out_shape=out,
        in_specs=[sm, vm],
        out_specs=vm,
        compiler_params=pltpu.CompilerParams(vmem_limit_bytes=8 << 20),
    )(at, came)
    return forward, back


def solution(mesh):
    fine = Mesh(mesh.devices.reshape(2, 8, 4, 2, 2, 2), ("xl", "z", "yh", "yl", "xh", "c"))
    ka, ga = ("xl", "z", "yh", "yl"), ("xh", "c")
    in_specs = (
        P(None, ka, None, None, ga),
        P(None, ka, None, None, ga),
        P(None, None, ka, ga),
        P(),
    )
    out_specs = (P(None, ka, None, ga), P(None, ka, None, ga))
    return jax.shard_map(local, mesh=fine, in_specs=in_specs, out_specs=out_specs, check_vma=False)
```

```python
import jax
import jax.numpy as jnp
from jax import lax
from jax.experimental import pallas as pl
from jax.experimental.pallas import tpu as pltpu
from jax.sharding import Mesh
from jax.sharding import PartitionSpec as P

NG = 1024
Q = 4
PAIR = 16
BLK = 128
NB = NG // BLK
SENT = 5
KQ = 6
BF = jnp.bfloat16
F32 = jnp.float32


def nt(left, right, precision=None):
    return lax.dot_general(
        left, right, (((1,), (1,)), ((), ())), preferred_element_type=F32, precision=precision
    )


def nn(left, right, precision=None):
    return jnp.dot(left, right, preferred_element_type=F32, precision=precision)


def fan(at_ref, w_ref, out_ref):
    lane = 0
    for xl in range(2):
        for d in range(SENT - xl):
            block = lax.rem(at_ref[0] + (4 * xl + d), NB)
            lanes = pl.ds(pl.multiple_of((block % 2) * BLK, BLK), BLK)
            out_ref[0, :, lane : lane + BLK] = w_ref[4 * xl + block // 2, :, lanes]
            lane += BLK
    piece = out_ref[0]
    for slot in range(1, 16):
        out_ref[slot, :, :] = piece


def fanned(at, w):
    vm = pl.BlockSpec(memory_space=pltpu.VMEM)
    return pl.pallas_call(
        fan,
        out_shape=jax.ShapeDtypeStruct((16, 8, (2 * SENT - 1) * BLK), BF),
        in_specs=[pl.BlockSpec(memory_space=pltpu.SMEM), vm],
        out_specs=vm,
        compiler_params=pltpu.CompilerParams(vmem_limit_bytes=16 << 20),
    )(at, w)


def weave(at_ref, *refs):
    pieces, out_ref = refs[:4], refs[4]
    for s in range(4):
        zl = at_ref[16] ^ (s // 2)
        yl = at_ref[3] ^ (s % 2)
        for i in range(16):
            out_ref[(i // 4) * 16 + zl * 8 + (i % 4) * 2 + yl, :, :] = pieces[s][i]


def woven(at, pieces):
    vm = pl.BlockSpec(memory_space=pltpu.VMEM)
    return pl.pallas_call(
        weave,
        out_shape=jax.ShapeDtypeStruct((64, 8, (2 * SENT - 1) * BLK), BF),
        in_specs=[pl.BlockSpec(memory_space=pltpu.SMEM)] + [vm] * 4,
        out_specs=vm,
        compiler_params=pltpu.CompilerParams(vmem_limit_bytes=16 << 20),
    )(at, *pieces)


def assemble(at_ref, *refs):
    pieces, (left_ref, flip_ref, val_ref) = refs[:4], refs[4:]
    x, core = at_ref[0], at_ref[1]
    minus = jnp.where(core == 0, 1.0, -1.0).astype(BF)
    for s in range(4):
        xl = (x ^ s) // 2
        for t in range(2):
            g = ((x ^ s) % 2) * 2 + (core ^ t)
            lanes = pl.ds(pl.multiple_of(g * 256, 256), 256)
            for j in range(3):
                row = xl * 96 + j * 32
                whole = pl.ds(pl.multiple_of(row, 32), 32)
                val_ref[whole, lanes] = pieces[s][1, t, j].reshape(32, 256)
                for r in range(2):
                    part = pl.ds(pl.multiple_of(row + (r ^ core) * PAIR, PAIR), PAIR)
                    piece = pieces[s][0, t, j, r]
                    if r == 0:
                        piece = piece * minus
                    left_ref[part, lanes] = piece
                    flip_ref[part, lanes] = piece * minus


def assembled(at, pieces):
    vm = pl.BlockSpec(memory_space=pltpu.VMEM)
    flat = jax.ShapeDtypeStruct((2 * KQ * PAIR, NG), BF)
    return pl.pallas_call(
        assemble,
        out_shape=(flat, flat, flat),
        in_specs=[pl.BlockSpec(memory_space=pltpu.SMEM)] + [vm] * 4,
        out_specs=(vm, vm, vm),
        compiler_params=pltpu.CompilerParams(vmem_limit_bytes=16 << 20),
        cost_estimate=pl.CostEstimate(flops=0, bytes_accessed=2_000_000, transcendentals=0),
    )(at, *pieces)


def stacked(w_ref, j):
    zero = jnp.zeros((BLK, BLK), BF)

    def block(b, d):
        half, i = b // 4, b % 4
        if d < 0 or d > 4 - half:
            return zero
        lane = half * SENT * BLK + d * BLK
        return w_ref[i * BLK : (i + 1) * BLK, lane : lane + BLK]

    first = j - 4 if j >= 4 else j - 3
    direct = jnp.concatenate(
        [
            jnp.concatenate([block(b % NB, j - b), block(b % NB, j + 1 - b)], 1)
            for b in range(first, j + 2)
        ],
        0,
    )
    width = 4 if j >= 4 else 5
    mirrored = jnp.concatenate(
        [
            jnp.concatenate([block(row, j + 1 + m - row) if j + 1 + m > row else zero for m in range(width)], 1)
            for row in (j, j + 1)
        ],
        0,
    )
    return first, direct, width, mirrored


def wrapped(x):
    return jnp.concatenate([x[:, 5 * BLK :], x, x[:, : 3 * BLK]], 1)


def screened_pair(w_ref, ahead, behind, j):
    def lanes(x, begin, count):
        return x[:, (begin + 3) * BLK : (begin + 3 + count) * BLK]

    first, direct, width, mirrored = stacked(w_ref, j)
    return nn(lanes(ahead, first, j + 2 - first), direct), nt(lanes(behind, j + 1, width), mirrored)


def contract_own(left_ref, flip_ref, own_ref, p_ref):
    left, flipped = wrapped(left_ref[...]), wrapped(flip_ref[...])
    for j in range(0, NB, 2):
        fore, back = screened_pair(own_ref, left, flipped, j)
        p_ref[:, j * BLK : (j + 2) * BLK] = fore + back


def contract(left_ref, flip_ref, val_ref, p_ref, oth_ref, out_ref):
    rows = left_ref.shape[0]
    half = rows // 2
    left, flipped = wrapped(left_ref[...]), wrapped(flip_ref[...])
    g1 = jnp.zeros((half, rows), F32)
    g2 = jnp.zeros((half, rows), F32)
    for j in range(0, NB, 2):
        columns = slice(j * BLK, (j + 2) * BLK)
        fore, back = screened_pair(oth_ref, flipped, left, j)
        q = (fore - back).reshape(KQ, 2, PAIR, 2 * BLK)
        p = p_ref[:, columns].reshape(KQ, 2, PAIR, 2 * BLK)
        x_real = (p[:, 0] + q[:, 1]).reshape(half, 2 * BLK).astype(BF)
        x_imag = (q[:, 0] - p[:, 1]).reshape(half, 2 * BLK).astype(BF)
        val = val_ref[:, columns]
        g1 += nt(x_real, val)
        g2 += nt(x_imag, val)
    r = lax.broadcasted_iota(jnp.int32, (half, rows), 0)
    c = lax.broadcasted_iota(jnp.int32, (half, rows), 1)
    same = r // PAIR == c // (2 * PAIR)
    g1 = jnp.where(same, g1, 0.0)
    g2 = jnp.where(same, g2, 0.0)
    c = lax.broadcasted_iota(jnp.int32, (rows, 128), 0)
    l = lax.broadcasted_iota(jnp.int32, (rows, 128), 1)
    hit = c % PAIR == l % PAIR
    part = (c // PAIR) % 2
    want = l // 64
    e1 = jnp.where(hit & (part == want), 1.0, 0.0)
    e2 = jnp.where(hit & (part != want), jnp.where(want == 0, -1.0, 1.0), 0.0)
    t = nn(g1, e1, lax.Precision.HIGHEST) + nn(g2, e2, lax.Precision.HIGHEST)
    r = lax.broadcasted_iota(jnp.int32, (half, 128), 0)
    l = lax.broadcasted_iota(jnp.int32, (half, 128), 1)
    t = jnp.where(r % 4 == (l // PAIR) % 4, t, 0.0)
    o = lax.broadcasted_iota(jnp.int32, (4 * 8, half), 0)
    r = lax.broadcasted_iota(jnp.int32, (4 * 8, half), 1)
    e3 = jnp.where((r // PAIR == o % 8) & ((r % PAIR) // 4 == o // 8), 1.0, 0.0)
    block = nn(e3, t, lax.Precision.HIGHEST)
    for slot in range(16):
        g = slot % 4
        out_ref[slot, :, :] = block[g * 8 : g * 8 + KQ, :]


def contracted(left, flipped, val, own):
    vm = pl.BlockSpec(memory_space=pltpu.VMEM)
    kept = pltpu.CompilerParams(vmem_limit_bytes=24 << 20)
    cost = pl.CostEstimate(flops=800_000_000, bytes_accessed=2_000_000, transcendentals=0)
    oth = lax.ppermute(own, "c", [(0, 1), (1, 0)])
    p = pl.pallas_call(
        contract_own,
        out_shape=jax.ShapeDtypeStruct((2 * KQ * PAIR, NG), F32),
        in_specs=[vm] * 3,
        out_specs=vm,
        compiler_params=kept,
        cost_estimate=cost,
    )(left, flipped, own)
    return pl.pallas_call(
        contract,
        out_shape=jax.ShapeDtypeStruct((16, KQ, 128), F32),
        in_specs=[vm] * 5,
        out_specs=vm,
        compiler_params=kept,
        cost_estimate=cost,
    )(left, flipped, val, p, oth)


def pick_rows(at_ref, got_ref, fwd_ref, pay_ref, row_ref):
    xl = at_ref[2]
    yl = at_ref[3]
    for q in range(Q):
        base = (q // 2) * 8 + (q % 2) * 2
        other = at_ref[4 + q]
        begin = at_ref[8 + q]
        for t in range(KQ):
            row = got_ref[base + yl * 4 + t // 3, pl.ds(xl * 3 + t % 3, 1), :]
            fwd_ref[q, pl.ds(t, 1), 0, :] = row[:, :64]
            fwd_ref[q, pl.ds(t, 1), 1, :] = row[:, 64:]
            col = lax.rem(begin + t, 12)
            slot = base + (col // 6) * 4 + (col % 6) // 3
            row_ref[pl.ds(q * KQ + t, 1), :] = got_ref[slot, pl.ds(other * 3 + col % 3, 1), :]
    pay = row_ref[...].astype(BF)
    for slot in range(32):
        pay_ref[slot, :, :] = pay


def pick_back(at_ref, came_ref, out_ref):
    for q in range(Q):
        rows = came_ref[at_ref[12 + q]].astype(F32)[q * KQ : (q + 1) * KQ, :]
        out_ref[q, :, 0, :] = rows[:, :64]
        out_ref[q, :, 1, :] = rows[:, 64:]


def local(cond, val, screened, k_plus):
    xl, yl, core = lax.axis_index("xl"), lax.axis_index("yl"), lax.axis_index("c")
    zh, zl, yh = lax.axis_index("zh"), lax.axis_index("zl"), lax.axis_index("yh")
    z = zh * 2 + zl
    w = lax.all_to_all(screened.reshape(8, 8, 256), ("xl", "xh", "c"), 0, 0)
    w = fanned(zh.astype(jnp.int32).reshape(1), w)
    w = lax.all_to_all(w, ("zh", "yh"), 0, 0)
    classes = [w]
    for s in range(1, 4):
        classes.append(lax.ppermute(w, ("zl", "yl"), [(i, i ^ s) for i in range(4)]))
    x = xl * 2 + lax.axis_index("xh")

    slots = [pairs.reshape(4, 2, 3, 2, PAIR, 256) for pairs in (cond, val)]
    keep = [lax.dynamic_index_in_dim(part, core, 1, False) for part in slots]
    given = [lax.dynamic_index_in_dim(part, 1 - core, 1, False) for part in slots]
    given = jnp.stack(given, 0)
    given = lax.ppermute(given, "c", [(0, 1), (1, 0)])
    pieces = []
    for s in range(4):
        both = [
            lax.dynamic_index_in_dim(part, x ^ s, 0, False)
            for part in (keep[0], given[0], keep[1], given[1])
        ]
        piece = jnp.stack(both, 0).reshape(2, 2, 3, 2, PAIR, 256)
        if s:
            piece = lax.ppermute(piece, ("xl", "xh"), [(i, i ^ s) for i in range(4)])
        pieces.append(piece)
    corner = k_plus[:, 0]
    row_step, col_step = corner // 12, corner % 12
    here = z * 4 + yh
    other = xl ^ ((here + row_step) // 32 % 2)
    begin = (6 * yl - col_step + 12) % 12
    source = (here - row_step) % 32
    at = jnp.concatenate([jnp.stack([x, core, xl, yl]), other, begin, source, zl[None]]).astype(jnp.int32)
    left, flipped, right = assembled(at, pieces)
    own = woven(at, classes).reshape(NG // 2, (2 * SENT - 1) * BLK)
    slots = contracted(left, flipped, right, own)
    got = lax.all_to_all(slots, ("xl", "yl", "xh", "c"), 0, 0)
    vm = pl.BlockSpec(memory_space=pltpu.VMEM)
    sm = pl.BlockSpec(memory_space=pltpu.SMEM)
    out = jax.ShapeDtypeStruct((Q, KQ, 2, 64), F32)
    forward, pay = pl.pallas_call(
        pick_rows,
        out_shape=(out, jax.ShapeDtypeStruct((32, Q * KQ, 128), BF)),
        in_specs=[sm, vm],
        out_specs=(vm, vm),
        scratch_shapes=[pltpu.VMEM((Q * KQ, 128), F32)],
        compiler_params=pltpu.CompilerParams(vmem_limit_bytes=8 << 20),
    )(at, got)
    came = lax.all_to_all(pay, ("zh", "zl", "yh"), 0, 0)
    back = pl.pallas_call(
        pick_back,
        out_shape=out,
        in_specs=[sm, vm],
        out_specs=vm,
        compiler_params=pltpu.CompilerParams(vmem_limit_bytes=8 << 20),
    )(at, came)
    return forward, back


def solution(mesh):
    fine = Mesh(mesh.devices.reshape(2, 4, 2, 4, 2, 2, 2), ("xl", "zh", "zl", "yh", "yl", "xh", "c"))
    ka, ga = ("xl", "zh", "zl", "yh", "yl"), ("xh", "c")
    in_specs = (
        P(None, ka, None, None, ga),
        P(None, ka, None, None, ga),
        P(None, None, ka, ga),
        P(),
    )
    out_specs = (P(None, ka, None, ga), P(None, ka, None, ga))
    return jax.shard_map(local, mesh=fine, in_specs=in_specs, out_specs=out_specs, check_vma=False)
```

```python
import jax
import jax.numpy as jnp
from jax import lax
from jax.experimental import pallas as pl
from jax.experimental.pallas import tpu as pltpu
from jax.sharding import Mesh
from jax.sharding import PartitionSpec as P

NG = 1024
Q = 4
PAIR = 16
BLK = 128
NB = NG // BLK
SENT = 5
KQ = 6
BF = jnp.bfloat16
F32 = jnp.float32


def nt(left, right, precision=None):
    return lax.dot_general(
        left, right, (((1,), (1,)), ((), ())), preferred_element_type=F32, precision=precision
    )


def nn(left, right, precision=None):
    return jnp.dot(left, right, preferred_element_type=F32, precision=precision)


def fan(at_ref, w_ref, out_ref):
    lane = 0
    for xl in range(2):
        for d in range(SENT - xl):
            block = lax.rem(at_ref[0] + (4 * xl + d), NB)
            lanes = pl.ds(pl.multiple_of((block % 2) * BLK, BLK), BLK)
            out_ref[0, :, lane : lane + BLK] = w_ref[4 * xl + block // 2, :, lanes]
            lane += BLK
    piece = out_ref[0]
    for slot in range(1, 64):
        out_ref[slot, :, :] = piece


def fanned(at, w):
    vm = pl.BlockSpec(memory_space=pltpu.VMEM)
    return pl.pallas_call(
        fan,
        out_shape=jax.ShapeDtypeStruct((64, 8, (2 * SENT - 1) * BLK), BF),
        in_specs=[pl.BlockSpec(memory_space=pltpu.SMEM), vm],
        out_specs=vm,
        compiler_params=pltpu.CompilerParams(vmem_limit_bytes=16 << 20),
    )(at, w)


def assemble(at_ref, *refs):
    pieces, (left_ref, flip_ref, val_ref) = refs[:4], refs[4:]
    x, core = at_ref[0], at_ref[1]
    minus = jnp.where(core == 0, 1.0, -1.0).astype(BF)
    for s in range(4):
        xl = (x ^ s) // 2
        for t in range(2):
            g = ((x ^ s) % 2) * 2 + (core ^ t)
            lanes = pl.ds(pl.multiple_of(g * 256, 256), 256)
            for j in range(3):
                row = xl * 96 + j * 32
                whole = pl.ds(pl.multiple_of(row, 32), 32)
                val_ref[whole, lanes] = pieces[s][1, t, j].reshape(32, 256)
                for r in range(2):
                    part = pl.ds(pl.multiple_of(row + (r ^ core) * PAIR, PAIR), PAIR)
                    piece = pieces[s][0, t, j, r]
                    if r == 0:
                        piece = piece * minus
                    left_ref[part, lanes] = piece
                    flip_ref[part, lanes] = piece * minus


def assembled(at, pieces):
    vm = pl.BlockSpec(memory_space=pltpu.VMEM)
    flat = jax.ShapeDtypeStruct((2 * KQ * PAIR, NG), BF)
    return pl.pallas_call(
        assemble,
        out_shape=(flat, flat, flat),
        in_specs=[pl.BlockSpec(memory_space=pltpu.SMEM)] + [vm] * 4,
        out_specs=(vm, vm, vm),
        compiler_params=pltpu.CompilerParams(vmem_limit_bytes=16 << 20),
        cost_estimate=pl.CostEstimate(flops=0, bytes_accessed=2_000_000, transcendentals=0),
    )(at, *pieces)


def stacked(w_ref, j):
    zero = jnp.zeros((BLK, BLK), BF)

    def block(b, d):
        half, i = b // 4, b % 4
        if d < 0 or d > 4 - half:
            return zero
        lane = half * SENT * BLK + d * BLK
        return w_ref[i * BLK : (i + 1) * BLK, lane : lane + BLK]

    first = j - 4 if j >= 4 else j - 3
    direct = jnp.concatenate(
        [
            jnp.concatenate([block(b % NB, j - b), block(b % NB, j + 1 - b)], 1)
            for b in range(first, j + 2)
        ],
        0,
    )
    width = 4 if j >= 4 else 5
    mirrored = jnp.concatenate(
        [
            jnp.concatenate([block(row, j + 1 + m - row) if j + 1 + m > row else zero for m in range(width)], 1)
            for row in (j, j + 1)
        ],
        0,
    )
    return first, direct, width, mirrored


def wrapped(x):
    return jnp.concatenate([x[:, 5 * BLK :], x, x[:, : 3 * BLK]], 1)


def screened_pair(w_ref, ahead, behind, j):
    def lanes(x, begin, count):
        return x[:, (begin + 3) * BLK : (begin + 3 + count) * BLK]

    first, direct, width, mirrored = stacked(w_ref, j)
    return nn(lanes(ahead, first, j + 2 - first), direct), nt(lanes(behind, j + 1, width), mirrored)


def contract_own(left_ref, flip_ref, own_ref, p_ref):
    left, flipped = wrapped(left_ref[...]), wrapped(flip_ref[...])
    for j in range(0, NB, 2):
        fore, back = screened_pair(own_ref, left, flipped, j)
        p_ref[:, j * BLK : (j + 2) * BLK] = fore + back


def contract(left_ref, flip_ref, val_ref, p_ref, oth_ref, out_ref):
    rows = left_ref.shape[0]
    half = rows // 2
    left, flipped = wrapped(left_ref[...]), wrapped(flip_ref[...])
    g1 = jnp.zeros((half, rows), F32)
    g2 = jnp.zeros((half, rows), F32)
    for j in range(0, NB, 2):
        columns = slice(j * BLK, (j + 2) * BLK)
        fore, back = screened_pair(oth_ref, flipped, left, j)
        q = (fore - back).reshape(KQ, 2, PAIR, 2 * BLK)
        p = p_ref[:, columns].reshape(KQ, 2, PAIR, 2 * BLK)
        x_real = (p[:, 0] + q[:, 1]).reshape(half, 2 * BLK).astype(BF)
        x_imag = (q[:, 0] - p[:, 1]).reshape(half, 2 * BLK).astype(BF)
        val = val_ref[:, columns]
        g1 += nt(x_real, val)
        g2 += nt(x_imag, val)
    r = lax.broadcasted_iota(jnp.int32, (half, rows), 0)
    c = lax.broadcasted_iota(jnp.int32, (half, rows), 1)
    same = r // PAIR == c // (2 * PAIR)
    g1 = jnp.where(same, g1, 0.0)
    g2 = jnp.where(same, g2, 0.0)
    c = lax.broadcasted_iota(jnp.int32, (rows, 128), 0)
    l = lax.broadcasted_iota(jnp.int32, (rows, 128), 1)
    hit = c % PAIR == l % PAIR
    part = (c // PAIR) % 2
    want = l // 64
    e1 = jnp.where(hit & (part == want), 1.0, 0.0)
    e2 = jnp.where(hit & (part != want), jnp.where(want == 0, -1.0, 1.0), 0.0)
    t = nn(g1, e1, lax.Precision.HIGHEST) + nn(g2, e2, lax.Precision.HIGHEST)
    r = lax.broadcasted_iota(jnp.int32, (half, 128), 0)
    l = lax.broadcasted_iota(jnp.int32, (half, 128), 1)
    t = jnp.where(r % 4 == (l // PAIR) % 4, t, 0.0)
    o = lax.broadcasted_iota(jnp.int32, (4 * 8, half), 0)
    r = lax.broadcasted_iota(jnp.int32, (4 * 8, half), 1)
    e3 = jnp.where((r // PAIR == o % 8) & ((r % PAIR) // 4 == o // 8), 1.0, 0.0)
    block = nn(e3, t, lax.Precision.HIGHEST)
    for slot in range(16):
        g = slot % 4
        out_ref[slot, :, :] = block[g * 8 : g * 8 + KQ, :]


def contracted(left, flipped, val, own):
    vm = pl.BlockSpec(memory_space=pltpu.VMEM)
    kept = pltpu.CompilerParams(vmem_limit_bytes=24 << 20)
    cost = pl.CostEstimate(flops=800_000_000, bytes_accessed=2_000_000, transcendentals=0)
    oth = lax.ppermute(own, "c", [(0, 1), (1, 0)])
    p = pl.pallas_call(
        contract_own,
        out_shape=jax.ShapeDtypeStruct((2 * KQ * PAIR, NG), F32),
        in_specs=[vm] * 3,
        out_specs=vm,
        compiler_params=kept,
        cost_estimate=cost,
    )(left, flipped, own)
    return pl.pallas_call(
        contract,
        out_shape=jax.ShapeDtypeStruct((16, KQ, 128), F32),
        in_specs=[vm] * 5,
        out_specs=vm,
        compiler_params=kept,
        cost_estimate=cost,
    )(left, flipped, val, p, oth)


def pick_rows(at_ref, got_ref, pay_ref, row_ref):
    for i in range(Q * KQ):
        row = got_ref[at_ref[2 + i], pl.ds(at_ref[2 + Q * KQ + i], 1), :]
        row_ref[pl.ds(i, 1), :] = row
    pay = row_ref[...].astype(BF)
    for slot in range(32):
        pay_ref[slot, :, :] = pay


def pick_forward(at_ref, got_ref, out_ref):
    last = 2 + 2 * Q * KQ + Q
    xl, yl = at_ref[last], at_ref[last + 1]
    for q in range(Q):
        base = (q // 2) * 8 + (q % 2) * 2 + yl * 4
        for c in range(2):
            rows = got_ref[base + c, pl.ds(xl * 3, 3), :]
            out_ref[q, c * 3 : c * 3 + 3, 0, :] = rows[:, :64]
            out_ref[q, c * 3 : c * 3 + 3, 1, :] = rows[:, 64:]


def pick_back(at_ref, came_ref, out_ref):
    for q in range(Q):
        rows = came_ref[at_ref[2 + 2 * Q * KQ + q]].astype(F32)[q * KQ : (q + 1) * KQ, :]
        out_ref[q, :, 0, :] = rows[:, :64]
        out_ref[q, :, 1, :] = rows[:, 64:]


def local(cond, val, screened, k_plus):
    xl, yl, core = lax.axis_index("xl"), lax.axis_index("yl"), lax.axis_index("c")
    z, yh = lax.axis_index("z"), lax.axis_index("yh")
    w = lax.all_to_all(screened.reshape(8, 8, 256), ("xl", "xh", "c"), 0, 0)
    w = fanned((z // 2).astype(jnp.int32).reshape(1), w)
    w = lax.all_to_all(w, ("z", "yh", "yl"), 0, 0)
    own = w.reshape(NG // 2, (2 * SENT - 1) * BLK)

    x = xl * 2 + lax.axis_index("xh")

    slots = [pairs.reshape(4, 2, 3, 2, PAIR, 256) for pairs in (cond, val)]
    keep = [lax.dynamic_index_in_dim(part, core, 1, False) for part in slots]
    given = [lax.dynamic_index_in_dim(part, 1 - core, 1, False) for part in slots]
    given = jnp.stack(given, 0)
    given = lax.ppermute(given, "c", [(0, 1), (1, 0)])
    pieces = []
    for s in range(4):
        both = [
            lax.dynamic_index_in_dim(part, x ^ s, 0, False)
            for part in (keep[0], given[0], keep[1], given[1])
        ]
        piece = jnp.stack(both, 0).reshape(2, 2, 3, 2, PAIR, 256)
        if s:
            piece = lax.ppermute(piece, ("xl", "xh"), [(i, i ^ s) for i in range(4)])
        pieces.append(piece)
    corner = k_plus[:, 0]
    row_step, col_step = corner // 12, corner % 12
    here = z * 4 + yh
    other = xl ^ ((here + row_step) // 32 % 2)
    begin = (6 * yl - col_step + 12) % 12
    source = (here - row_step) % 32
    col = (begin[:, None] + jnp.arange(KQ)) % 12
    base = jnp.array([0, 2, 8, 10])[:, None]
    slot = base + col // 6 * 4 + col % 6 // 3
    row = other[:, None] * 3 + col % 3
    parts = [jnp.stack([x, core]), slot.reshape(-1), row.reshape(-1), source, jnp.stack([xl, yl])]
    at = jnp.concatenate(parts).astype(jnp.int32)
    left, flipped, right = assembled(at, pieces)
    slots = contracted(left, flipped, right, own)
    got = lax.all_to_all(slots, ("xl", "yl", "xh", "c"), 0, 0)
    vm = pl.BlockSpec(memory_space=pltpu.VMEM)
    sm = pl.BlockSpec(memory_space=pltpu.SMEM)
    out = jax.ShapeDtypeStruct((Q, KQ, 2, 64), F32)
    kept = pltpu.CompilerParams(vmem_limit_bytes=8 << 20)
    pay = pl.pallas_call(
        pick_rows,
        out_shape=jax.ShapeDtypeStruct((32, Q * KQ, 128), BF),
        in_specs=[sm, vm],
        out_specs=vm,
        scratch_shapes=[pltpu.VMEM((Q * KQ, 128), F32)],
        compiler_params=kept,
    )(at, got)
    came = lax.all_to_all(pay, ("z", "yh"), 0, 0)
    forward = pl.pallas_call(
        pick_forward, out_shape=out, in_specs=[sm, vm], out_specs=vm, compiler_params=kept
    )(at, got)
    back = pl.pallas_call(
        pick_back,
        out_shape=out,
        in_specs=[sm, vm],
        out_specs=vm,
        compiler_params=pltpu.CompilerParams(vmem_limit_bytes=8 << 20),
    )(at, came)
    return forward, back


def solution(mesh):
    fine = Mesh(mesh.devices.reshape(2, 8, 4, 2, 2, 2), ("xl", "z", "yh", "yl", "xh", "c"))
    ka, ga = ("xl", "z", "yh", "yl"), ("xh", "c")
    in_specs = (
        P(None, ka, None, None, ga),
        P(None, ka, None, None, ga),
        P(None, None, ka, ga),
        P(),
    )
    out_specs = (P(None, ka, None, ga), P(None, ka, None, ga))
    return jax.shard_map(local, mesh=fine, in_specs=in_specs, out_specs=out_specs, check_vma=False)
```

```python
import jax
import jax.numpy as jnp
from jax import lax
from jax.experimental import pallas as pl
from jax.experimental.pallas import tpu as pltpu
from jax.sharding import Mesh
from jax.sharding import PartitionSpec as P

NG = 1024
Q = 4
PAIR = 16
BLK = 128
NB = NG // BLK
SENT = 5
KQ = 6
BF = jnp.bfloat16
F32 = jnp.float32


def nt(left, right):
    return lax.dot_general(left, right, (((1,), (1,)), ((), ())), preferred_element_type=F32)


def nn(left, right):
    return jnp.dot(left, right, preferred_element_type=F32)


def exact_terms(x, axis):
    high = x.astype(BF)
    rest = x - high.astype(F32)
    middle = rest.astype(BF)
    low = (rest - middle.astype(F32)).astype(BF)
    return jnp.concatenate([high, middle, low], axis)


def fan(at_ref, w_ref, out_ref):
    lane = 0
    for xl in range(2):
        for d in range(SENT - xl):
            block = lax.rem(at_ref[0] + (4 * xl + d), NB)
            lanes = pl.ds(pl.multiple_of((block % 2) * BLK, BLK), BLK)
            out_ref[0, :, lane : lane + BLK] = w_ref[4 * xl + block // 2, :, lanes]
            lane += BLK
    piece = out_ref[0]
    for slot in range(1, 64):
        out_ref[slot, :, :] = piece


def fanned(at, w):
    vm = pl.BlockSpec(memory_space=pltpu.VMEM)
    return pl.pallas_call(
        fan,
        out_shape=jax.ShapeDtypeStruct((64, 8, (2 * SENT - 1) * BLK), BF),
        in_specs=[pl.BlockSpec(memory_space=pltpu.SMEM), vm],
        out_specs=vm,
        compiler_params=pltpu.CompilerParams(vmem_limit_bytes=16 << 20),
    )(at, w)


def assemble(at_ref, *refs):
    pieces, (left_ref, flip_ref, val_ref) = refs[:4], refs[4:]
    x, core = at_ref[0], at_ref[1]
    minus = jnp.where(core == 0, 1.0, -1.0).astype(BF)
    for s in range(4):
        xl = (x ^ s) // 2
        for t in range(2):
            g = ((x ^ s) % 2) * 2 + (core ^ t)
            lanes = pl.ds(pl.multiple_of(g * 256, 256), 256)
            for j in range(3):
                row = xl * 96 + j * 32
                whole = pl.ds(pl.multiple_of(row, 32), 32)
                val_ref[whole, lanes] = pieces[s][1, t, j].reshape(32, 256)
                for r in range(2):
                    part = pl.ds(pl.multiple_of(row + (r ^ core) * PAIR, PAIR), PAIR)
                    piece = pieces[s][0, t, j, r]
                    if r == 0:
                        piece = piece * minus
                    left_ref[part, lanes] = piece
                    flip_ref[part, lanes] = piece * minus


def assembled(at, pieces):
    vm = pl.BlockSpec(memory_space=pltpu.VMEM)
    flat = jax.ShapeDtypeStruct((2 * KQ * PAIR, NG), BF)
    return pl.pallas_call(
        assemble,
        out_shape=(flat, flat, flat),
        in_specs=[pl.BlockSpec(memory_space=pltpu.SMEM)] + [vm] * 4,
        out_specs=(vm, vm, vm),
        compiler_params=pltpu.CompilerParams(vmem_limit_bytes=16 << 20),
        cost_estimate=pl.CostEstimate(flops=0, bytes_accessed=2_000_000, transcendentals=0),
    )(at, *pieces)


def stacked(w_ref, j):
    zero = jnp.zeros((BLK, BLK), BF)

    def block(b, d):
        half, i = b // 4, b % 4
        if d < 0 or d > 4 - half:
            return zero
        lane = half * SENT * BLK + d * BLK
        return w_ref[i * BLK : (i + 1) * BLK, lane : lane + BLK]

    first = j - 4 if j >= 4 else j - 3
    direct = jnp.concatenate(
        [
            jnp.concatenate([block(b % NB, j - b), block(b % NB, j + 1 - b)], 1)
            for b in range(first, j + 2)
        ],
        0,
    )
    width = 4 if j >= 4 else 5
    mirrored = jnp.concatenate(
        [
            jnp.concatenate([block(row, j + 1 + m - row) if j + 1 + m > row else zero for m in range(width)], 1)
            for row in (j, j + 1)
        ],
        0,
    )
    return first, direct, width, mirrored


def wrapped(x):
    return jnp.concatenate([x[:, 5 * BLK :], x, x[:, : 3 * BLK]], 1)


def screened_pair(w_ref, ahead, behind, j):
    def lanes(x, begin, count):
        return x[:, (begin + 3) * BLK : (begin + 3 + count) * BLK]

    first, direct, width, mirrored = stacked(w_ref, j)
    return nn(lanes(ahead, first, j + 2 - first), direct), nt(lanes(behind, j + 1, width), mirrored)


def contract_own(left_ref, flip_ref, own_ref, p_ref):
    left, flipped = wrapped(left_ref[...]), wrapped(flip_ref[...])
    for j in range(0, NB, 2):
        fore, back = screened_pair(own_ref, left, flipped, j)
        p_ref[:, j * BLK : (j + 2) * BLK] = fore + back


def contract(left_ref, flip_ref, val_ref, p_ref, oth_ref, out_ref):
    rows = left_ref.shape[0]
    half = rows // 2
    left, flipped = wrapped(left_ref[...]), wrapped(flip_ref[...])
    g1 = jnp.zeros((half, rows), F32)
    g2 = jnp.zeros((half, rows), F32)
    for j in range(0, NB, 2):
        columns = slice(j * BLK, (j + 2) * BLK)
        fore, back = screened_pair(oth_ref, flipped, left, j)
        q = (fore - back).reshape(KQ, 2, PAIR, 2 * BLK)
        p = p_ref[:, columns].reshape(KQ, 2, PAIR, 2 * BLK)
        x_real = (p[:, 0] + q[:, 1]).reshape(half, 2 * BLK).astype(BF)
        x_imag = (q[:, 0] - p[:, 1]).reshape(half, 2 * BLK).astype(BF)
        val = val_ref[:, columns]
        g1 += nt(x_real, val)
        g2 += nt(x_imag, val)
    r = lax.broadcasted_iota(jnp.int32, (half, rows), 0)
    c = lax.broadcasted_iota(jnp.int32, (half, rows), 1)
    same = (r >> 4) == (c >> 5)
    both = jnp.concatenate([jnp.where(same, g1, 0.0), jnp.where(same, g2, 0.0)], 1)
    c = lax.broadcasted_iota(jnp.int32, (rows, 128), 0)
    l = lax.broadcasted_iota(jnp.int32, (rows, 128), 1)
    hit = (c & 15) == (l & 15)
    part = (c >> 4) & 1
    want = l >> 6
    e1 = jnp.where(hit & (part == want), 1.0, 0.0)
    e2 = jnp.where(hit & (part != want), jnp.where(want == 0, -1.0, 1.0), 0.0)
    e12 = jnp.concatenate([e1, e2], 0).astype(BF)
    t = nn(exact_terms(both, 1), jnp.concatenate([e12] * 3, 0))
    r = lax.broadcasted_iota(jnp.int32, (half, 128), 0)
    l = lax.broadcasted_iota(jnp.int32, (half, 128), 1)
    t = jnp.where((r & 3) == ((l >> 4) & 3), t, 0.0)
    o = lax.broadcasted_iota(jnp.int32, (4 * 8, half), 0)
    r = lax.broadcasted_iota(jnp.int32, (4 * 8, half), 1)
    e3 = jnp.where(((r >> 4) == (o & 7)) & (((r & 15) >> 2) == (o >> 3)), 1.0, 0.0).astype(BF)
    block = nn(jnp.concatenate([e3] * 3, 1), exact_terms(t, 0))
    for slot in range(16):
        g = slot % 4
        out_ref[slot, :, :] = block[g * 8 : g * 8 + KQ, :]


def contracted(left, flipped, val, own):
    vm = pl.BlockSpec(memory_space=pltpu.VMEM)
    kept = pltpu.CompilerParams(vmem_limit_bytes=24 << 20)
    cost = pl.CostEstimate(flops=800_000_000, bytes_accessed=2_000_000, transcendentals=0)
    oth = lax.ppermute(own, "c", [(0, 1), (1, 0)])
    p = pl.pallas_call(
        contract_own,
        out_shape=jax.ShapeDtypeStruct((2 * KQ * PAIR, NG), F32),
        in_specs=[vm] * 3,
        out_specs=vm,
        compiler_params=kept,
        cost_estimate=cost,
    )(left, flipped, own)
    return pl.pallas_call(
        contract,
        out_shape=jax.ShapeDtypeStruct((16, KQ, 128), F32),
        in_specs=[vm] * 5,
        out_specs=vm,
        compiler_params=kept,
        cost_estimate=cost,
    )(left, flipped, val, p, oth)


def pick_rows(at_ref, got_ref, pay_ref, row_ref):
    for i in range(Q * KQ):
        row = got_ref[at_ref[2 + i], pl.ds(at_ref[2 + Q * KQ + i], 1), :]
        row_ref[pl.ds(i, 1), :] = row
    pay = row_ref[...].astype(BF)
    for slot in range(32):
        pay_ref[slot, :, :] = pay


def pick_forward(at_ref, got_ref, out_ref):
    last = 2 + 2 * Q * KQ + Q
    xl, yl = at_ref[last], at_ref[last + 1]
    for q in range(Q):
        base = (q // 2) * 8 + (q % 2) * 2 + yl * 4
        for c in range(2):
            rows = got_ref[base + c, pl.ds(xl * 3, 3), :]
            out_ref[q, c * 3 : c * 3 + 3, 0, :] = rows[:, :64]
            out_ref[q, c * 3 : c * 3 + 3, 1, :] = rows[:, 64:]


def pick_back(at_ref, came_ref, out_ref):
    for q in range(Q):
        rows = came_ref[at_ref[2 + 2 * Q * KQ + q]].astype(F32)[q * KQ : (q + 1) * KQ, :]
        out_ref[q, :, 0, :] = rows[:, :64]
        out_ref[q, :, 1, :] = rows[:, 64:]


def local(cond, val, screened, k_plus):
    xl, yl, core = lax.axis_index("xl"), lax.axis_index("yl"), lax.axis_index("c")
    z, yh = lax.axis_index("z"), lax.axis_index("yh")
    w = lax.all_to_all(screened.reshape(8, 8, 256), ("xl", "xh", "c"), 0, 0)
    w = fanned((z // 2).astype(jnp.int32).reshape(1), w)
    w = lax.all_to_all(w, ("z", "yh", "yl"), 0, 0)
    own = w.reshape(NG // 2, (2 * SENT - 1) * BLK)

    x = xl * 2 + lax.axis_index("xh")

    slots = [pairs.reshape(4, 2, 3, 2, PAIR, 256) for pairs in (cond, val)]
    keep = [lax.dynamic_index_in_dim(part, core, 1, False) for part in slots]
    given = [lax.dynamic_index_in_dim(part, 1 - core, 1, False) for part in slots]
    given = jnp.stack(given, 0)
    given = lax.ppermute(given, "c", [(0, 1), (1, 0)])
    pieces = []
    for s in range(4):
        both = [
            lax.dynamic_index_in_dim(part, x ^ s, 0, False)
            for part in (keep[0], given[0], keep[1], given[1])
        ]
        piece = jnp.stack(both, 0).reshape(2, 2, 3, 2, PAIR, 256)
        if s:
            piece = lax.ppermute(piece, ("xl", "xh"), [(i, i ^ s) for i in range(4)])
        pieces.append(piece)
    corner = k_plus[:, 0]
    row_step, col_step = corner // 12, corner % 12
    here = z * 4 + yh
    other = xl ^ ((here + row_step) // 32 % 2)
    begin = (6 * yl - col_step + 12) % 12
    source = (here - row_step) % 32
    col = (begin[:, None] + jnp.arange(KQ)) % 12
    base = jnp.array([0, 2, 8, 10])[:, None]
    slot = base + col // 6 * 4 + col % 6 // 3
    row = other[:, None] * 3 + col % 3
    parts = [jnp.stack([x, core]), slot.reshape(-1), row.reshape(-1), source, jnp.stack([xl, yl])]
    at = jnp.concatenate(parts).astype(jnp.int32)
    left, flipped, right = assembled(at, pieces)
    slots = contracted(left, flipped, right, own)
    got = lax.all_to_all(slots, ("xl", "yl", "xh", "c"), 0, 0)
    vm = pl.BlockSpec(memory_space=pltpu.VMEM)
    sm = pl.BlockSpec(memory_space=pltpu.SMEM)
    out = jax.ShapeDtypeStruct((Q, KQ, 2, 64), F32)
    kept = pltpu.CompilerParams(vmem_limit_bytes=8 << 20)
    pay = pl.pallas_call(
        pick_rows,
        out_shape=jax.ShapeDtypeStruct((32, Q * KQ, 128), BF),
        in_specs=[sm, vm],
        out_specs=vm,
        scratch_shapes=[pltpu.VMEM((Q * KQ, 128), F32)],
        compiler_params=kept,
    )(at, got)
    came = lax.all_to_all(pay, ("z", "yh"), 0, 0)
    forward = pl.pallas_call(
        pick_forward, out_shape=out, in_specs=[sm, vm], out_specs=vm, compiler_params=kept
    )(at, got)
    back = pl.pallas_call(
        pick_back,
        out_shape=out,
        in_specs=[sm, vm],
        out_specs=vm,
        compiler_params=pltpu.CompilerParams(vmem_limit_bytes=8 << 20),
    )(at, came)
    return forward, back


def solution(mesh):
    fine = Mesh(mesh.devices.reshape(2, 8, 4, 2, 2, 2), ("xl", "z", "yh", "yl", "xh", "c"))
    ka, ga = ("xl", "z", "yh", "yl"), ("xh", "c")
    in_specs = (
        P(None, ka, None, None, ga),
        P(None, ka, None, None, ga),
        P(None, None, ka, ga),
        P(),
    )
    out_specs = (P(None, ka, None, ga), P(None, ka, None, ga))
    return jax.shard_map(local, mesh=fine, in_specs=in_specs, out_specs=out_specs, check_vma=False)
```

```python
import jax
import jax.numpy as jnp
from jax import lax
from jax.experimental import pallas as pl
from jax.experimental.pallas import tpu as pltpu
from jax.sharding import Mesh
from jax.sharding import PartitionSpec as P

NG = 1024
Q = 4
PAIR = 16
BLK = 128
NB = NG // BLK
SENT = 5
KQ = 6
BF = jnp.bfloat16
F32 = jnp.float32


def nt(left, right, precision=None):
    return lax.dot_general(
        left, right, (((1,), (1,)), ((), ())), preferred_element_type=F32, precision=precision
    )


def nn(left, right, precision=None):
    return jnp.dot(left, right, preferred_element_type=F32, precision=precision)


def fan(at_ref, w_ref, out_ref):
    lane = 0
    for xl in range(2):
        for d in range(SENT - xl):
            block = lax.rem(at_ref[0] + (4 * xl + d), NB)
            lanes = pl.ds(pl.multiple_of((block % 2) * BLK, BLK), BLK)
            out_ref[0, :, lane : lane + BLK] = w_ref[4 * xl + block // 2, :, lanes]
            lane += BLK
    piece = out_ref[0]
    for slot in range(1, 64):
        out_ref[slot, :, :] = piece


def fanned(at, w):
    vm = pl.BlockSpec(memory_space=pltpu.VMEM)
    return pl.pallas_call(
        fan,
        out_shape=jax.ShapeDtypeStruct((64, 8, (2 * SENT - 1) * BLK), BF),
        in_specs=[pl.BlockSpec(memory_space=pltpu.SMEM), vm],
        out_specs=vm,
        compiler_params=pltpu.CompilerParams(vmem_limit_bytes=16 << 20),
    )(at, w)


def assemble(at_ref, *refs):
    pieces, (left_ref, flip_ref, val_ref) = refs[:4], refs[4:]
    x, core = at_ref[0], at_ref[1]
    minus = jnp.where(core == 0, 1.0, -1.0).astype(BF)
    for s in range(4):
        xl = (x ^ s) // 2
        for t in range(2):
            g = ((x ^ s) % 2) * 2 + (core ^ t)
            lanes = pl.ds(pl.multiple_of(g * 256, 256), 256)
            for j in range(3):
                row = xl * 96 + j * 32
                whole = pl.ds(pl.multiple_of(row, 32), 32)
                val_ref[whole, lanes] = pieces[s][1, t, j].reshape(32, 256)
                for r in range(2):
                    part = pl.ds(pl.multiple_of(row + (r ^ core) * PAIR, PAIR), PAIR)
                    piece = pieces[s][0, t, j, r]
                    if r == 0:
                        piece = piece * minus
                    left_ref[part, lanes] = piece
                    flip_ref[part, lanes] = piece * minus


def assembled(at, pieces):
    vm = pl.BlockSpec(memory_space=pltpu.VMEM)
    flat = jax.ShapeDtypeStruct((2 * KQ * PAIR, NG), BF)
    return pl.pallas_call(
        assemble,
        out_shape=(flat, flat, flat),
        in_specs=[pl.BlockSpec(memory_space=pltpu.SMEM)] + [vm] * 4,
        out_specs=(vm, vm, vm),
        compiler_params=pltpu.CompilerParams(vmem_limit_bytes=16 << 20),
        cost_estimate=pl.CostEstimate(flops=0, bytes_accessed=2_000_000, transcendentals=0),
    )(at, *pieces)


def stacked(w_ref, j):
    zero = jnp.zeros((BLK, BLK), BF)

    def block(b, d):
        half, i = b // 4, b % 4
        if d < 0 or d > 4 - half:
            return zero
        lane = half * SENT * BLK + d * BLK
        starts = [yh * 128 + i * 32 + zl * 16 for zl in range(2) for yh in range(4)]
        return jnp.concatenate([w_ref[at : at + 16, lane : lane + BLK] for at in starts], 0)

    first = j - 4 if j >= 4 else j - 3
    direct = jnp.concatenate(
        [
            jnp.concatenate([block(b % NB, j - b), block(b % NB, j + 1 - b)], 1)
            for b in range(first, j + 2)
        ],
        0,
    )
    width = 4 if j >= 4 else 5
    mirrored = jnp.concatenate(
        [
            jnp.concatenate([block(row, j + 1 + m - row) if j + 1 + m > row else zero for m in range(width)], 1)
            for row in (j, j + 1)
        ],
        0,
    )
    return first, direct, width, mirrored


def wrapped(x):
    return jnp.concatenate([x[:, 5 * BLK :], x, x[:, : 3 * BLK]], 1)


def screened_pair(w_ref, ahead, behind, j):
    def lanes(x, begin, count):
        return x[:, (begin + 3) * BLK : (begin + 3 + count) * BLK]

    first, direct, width, mirrored = stacked(w_ref, j)
    return nn(lanes(ahead, first, j + 2 - first), direct), nt(lanes(behind, j + 1, width), mirrored)


def contract_own(left_ref, flip_ref, own_ref, p_ref):
    left, flipped = wrapped(left_ref[...]), wrapped(flip_ref[...])
    for j in range(0, NB, 2):
        fore, back = screened_pair(own_ref, left, flipped, j)
        p_ref[:, j * BLK : (j + 2) * BLK] = fore + back


def contract(left_ref, flip_ref, val_ref, p_ref, oth_ref, out_ref):
    rows = left_ref.shape[0]
    half = rows // 2
    left, flipped = wrapped(left_ref[...]), wrapped(flip_ref[...])
    g1 = jnp.zeros((half, rows), F32)
    g2 = jnp.zeros((half, rows), F32)
    for j in range(0, NB, 2):
        columns = slice(j * BLK, (j + 2) * BLK)
        fore, back = screened_pair(oth_ref, flipped, left, j)
        q = (fore - back).reshape(KQ, 2, PAIR, 2 * BLK)
        p = p_ref[:, columns].reshape(KQ, 2, PAIR, 2 * BLK)
        x_real = (p[:, 0] + q[:, 1]).reshape(half, 2 * BLK).astype(BF)
        x_imag = (q[:, 0] - p[:, 1]).reshape(half, 2 * BLK).astype(BF)
        val = val_ref[:, columns]
        g1 += nt(x_real, val)
        g2 += nt(x_imag, val)
    r = lax.broadcasted_iota(jnp.int32, (half, rows), 0)
    c = lax.broadcasted_iota(jnp.int32, (half, rows), 1)
    same = r // PAIR == c // (2 * PAIR)
    g1 = jnp.where(same, g1, 0.0)
    g2 = jnp.where(same, g2, 0.0)
    c = lax.broadcasted_iota(jnp.int32, (rows, 128), 0)
    l = lax.broadcasted_iota(jnp.int32, (rows, 128), 1)
    hit = c % PAIR == l % PAIR
    part = (c // PAIR) % 2
    want = l // 64
    e1 = jnp.where(hit & (part == want), 1.0, 0.0)
    e2 = jnp.where(hit & (part != want), jnp.where(want == 0, -1.0, 1.0), 0.0)
    t = nn(g1, e1, lax.Precision.HIGHEST) + nn(g2, e2, lax.Precision.HIGHEST)
    r = lax.broadcasted_iota(jnp.int32, (half, 128), 0)
    l = lax.broadcasted_iota(jnp.int32, (half, 128), 1)
    t = jnp.where(r % 4 == (l // PAIR) % 4, t, 0.0)
    o = lax.broadcasted_iota(jnp.int32, (4 * 8, half), 0)
    r = lax.broadcasted_iota(jnp.int32, (4 * 8, half), 1)
    e3 = jnp.where((r // PAIR == o % 8) & ((r % PAIR) // 4 == o // 8), 1.0, 0.0)
    block = nn(e3, t, lax.Precision.HIGHEST)
    for slot in range(16):
        g = slot % 4
        out_ref[slot, :, :] = block[g * 8 : g * 8 + KQ, :]


def contracted(left, flipped, val, own):
    vm = pl.BlockSpec(memory_space=pltpu.VMEM)
    kept = pltpu.CompilerParams(vmem_limit_bytes=24 << 20)
    cost = pl.CostEstimate(flops=800_000_000, bytes_accessed=2_000_000, transcendentals=0)
    oth = lax.ppermute(own, "c", [(0, 1), (1, 0)])
    p = pl.pallas_call(
        contract_own,
        out_shape=jax.ShapeDtypeStruct((2 * KQ * PAIR, NG), F32),
        in_specs=[vm] * 3,
        out_specs=vm,
        compiler_params=kept,
        cost_estimate=cost,
    )(left, flipped, own)
    return pl.pallas_call(
        contract,
        out_shape=jax.ShapeDtypeStruct((16, KQ, 128), F32),
        in_specs=[vm] * 5,
        out_specs=vm,
        compiler_params=kept,
        cost_estimate=cost,
    )(left, flipped, val, p, oth)


def pick_rows(at_ref, got_ref, pay_ref, row_ref):
    for i in range(Q * KQ):
        row = got_ref[at_ref[2 + i], pl.ds(at_ref[2 + Q * KQ + i], 1), :]
        row_ref[pl.ds(i, 1), :] = row
    pay = row_ref[...].astype(BF)
    for slot in range(32):
        pay_ref[slot, :, :] = pay


def pick_forward(at_ref, got_ref, out_ref):
    last = 2 + 2 * Q * KQ + Q
    xl, yl = at_ref[last], at_ref[last + 1]
    for q in range(Q):
        base = (q // 2) * 8 + (q % 2) * 2 + yl * 4
        for c in range(2):
            rows = got_ref[base + c, pl.ds(xl * 3, 3), :]
            out_ref[q, c * 3 : c * 3 + 3, 0, :] = rows[:, :64]
            out_ref[q, c * 3 : c * 3 + 3, 1, :] = rows[:, 64:]


def pick_back(at_ref, came_ref, out_ref):
    for q in range(Q):
        rows = came_ref[at_ref[2 + 2 * Q * KQ + q]].astype(F32)[q * KQ : (q + 1) * KQ, :]
        out_ref[q, :, 0, :] = rows[:, :64]
        out_ref[q, :, 1, :] = rows[:, 64:]


def local(cond, val, screened, k_plus):
    xl, yl, core = lax.axis_index("xl"), lax.axis_index("yl"), lax.axis_index("c")
    z, yh = lax.axis_index("z"), lax.axis_index("yh")
    w = lax.all_to_all(screened.reshape(8, 8, 256), ("xl", "xh", "c"), 0, 0)
    w = fanned((z // 2).astype(jnp.int32).reshape(1), w)
    w = lax.all_to_all(w, ("yh", "z", "yl"), 0, 0)
    own = w.reshape(NG // 2, (2 * SENT - 1) * BLK)

    x = xl * 2 + lax.axis_index("xh")

    slots = [pairs.reshape(4, 2, 3, 2, PAIR, 256) for pairs in (cond, val)]
    keep = [lax.dynamic_index_in_dim(part, core, 1, False) for part in slots]
    given = [lax.dynamic_index_in_dim(part, 1 - core, 1, False) for part in slots]
    given = jnp.stack(given, 0)
    given = lax.ppermute(given, "c", [(0, 1), (1, 0)])
    pieces = []
    for s in range(4):
        both = [
            lax.dynamic_index_in_dim(part, x ^ s, 0, False)
            for part in (keep[0], given[0], keep[1], given[1])
        ]
        piece = jnp.stack(both, 0).reshape(2, 2, 3, 2, PAIR, 256)
        if s:
            piece = lax.ppermute(piece, ("xl", "xh"), [(i, i ^ s) for i in range(4)])
        pieces.append(piece)
    corner = k_plus[:, 0]
    row_step, col_step = corner // 12, corner % 12
    here = z * 4 + yh
    other = xl ^ ((here + row_step) // 32 % 2)
    begin = (6 * yl - col_step + 12) % 12
    source = (here - row_step) % 32
    source = source % 4 * 8 + source // 4
    col = (begin[:, None] + jnp.arange(KQ)) % 12
    base = jnp.array([0, 2, 8, 10])[:, None]
    slot = base + col // 6 * 4 + col % 6 // 3
    row = other[:, None] * 3 + col % 3
    parts = [jnp.stack([x, core]), slot.reshape(-1), row.reshape(-1), source, jnp.stack([xl, yl])]
    at = jnp.concatenate(parts).astype(jnp.int32)
    left, flipped, right = assembled(at, pieces)
    slots = contracted(left, flipped, right, own)
    got = lax.all_to_all(slots, ("xl", "yl", "xh", "c"), 0, 0)
    vm = pl.BlockSpec(memory_space=pltpu.VMEM)
    sm = pl.BlockSpec(memory_space=pltpu.SMEM)
    out = jax.ShapeDtypeStruct((Q, KQ, 2, 64), F32)
    kept = pltpu.CompilerParams(vmem_limit_bytes=8 << 20)
    pay = pl.pallas_call(
        pick_rows,
        out_shape=jax.ShapeDtypeStruct((32, Q * KQ, 128), BF),
        in_specs=[sm, vm],
        out_specs=vm,
        scratch_shapes=[pltpu.VMEM((Q * KQ, 128), F32)],
        compiler_params=kept,
    )(at, got)
    came = lax.all_to_all(pay, ("yh", "z"), 0, 0)
    forward = pl.pallas_call(
        pick_forward, out_shape=out, in_specs=[sm, vm], out_specs=vm, compiler_params=kept
    )(at, got)
    back = pl.pallas_call(
        pick_back,
        out_shape=out,
        in_specs=[sm, vm],
        out_specs=vm,
        compiler_params=pltpu.CompilerParams(vmem_limit_bytes=8 << 20),
    )(at, came)
    return forward, back


def solution(mesh):
    fine = Mesh(mesh.devices.reshape(2, 8, 4, 2, 2, 2), ("xl", "z", "yh", "yl", "xh", "c"))
    ka, ga = ("xl", "z", "yh", "yl"), ("xh", "c")
    in_specs = (
        P(None, ka, None, None, ga),
        P(None, ka, None, None, ga),
        P(None, None, ka, ga),
        P(),
    )
    out_specs = (P(None, ka, None, ga), P(None, ka, None, ga))
    return jax.shard_map(local, mesh=fine, in_specs=in_specs, out_specs=out_specs, check_vma=False)
```

```python
import jax
import jax.numpy as jnp
from jax import lax
from jax.experimental import pallas as pl
from jax.experimental.pallas import tpu as pltpu
from jax.sharding import Mesh
from jax.sharding import PartitionSpec as P

NG = 1024
Q = 4
PAIR = 16
BLK = 128
NB = NG // BLK
SENT = 5
KQ = 6
BF = jnp.bfloat16
F32 = jnp.float32


def nt(left, right, precision=None):
    return lax.dot_general(
        left, right, (((1,), (1,)), ((), ())), preferred_element_type=F32, precision=precision
    )


def nn(left, right, precision=None):
    return jnp.dot(left, right, preferred_element_type=F32, precision=precision)


def fan(at_ref, w_ref, out_ref):
    lane = 0
    for xl in range(2):
        for d in range(SENT - xl):
            block = lax.rem(at_ref[0] + (4 * xl + d), NB)
            lanes = pl.ds(pl.multiple_of((block % 2) * BLK, BLK), BLK)
            out_ref[0, :, lane : lane + BLK] = w_ref[4 * xl + block // 2, :, lanes]
            lane += BLK
    piece = out_ref[0]
    for slot in range(1, 64):
        out_ref[slot, :, :] = piece


def fanned(at, w):
    vm = pl.BlockSpec(memory_space=pltpu.VMEM)
    return pl.pallas_call(
        fan,
        out_shape=jax.ShapeDtypeStruct((64, 8, (2 * SENT - 1) * BLK), BF),
        in_specs=[pl.BlockSpec(memory_space=pltpu.SMEM), vm],
        out_specs=vm,
        compiler_params=pltpu.CompilerParams(vmem_limit_bytes=16 << 20),
    )(at, w)


def assemble(at_ref, *refs):
    pieces, (left_ref, flip_ref, val_ref) = refs[:4], refs[4:]
    x, core = at_ref[0], at_ref[1]
    minus = jnp.where(core == 0, 1.0, -1.0).astype(BF)
    for s in range(4):
        xl = (x ^ s) // 2
        for t in range(2):
            g = ((x ^ s) % 2) * 2 + (core ^ t)
            lanes = pl.ds(pl.multiple_of(g * 256, 256), 256)
            for j in range(3):
                row = xl * 96 + j * 32
                whole = pl.ds(pl.multiple_of(row, 32), 32)
                val_ref[whole, lanes] = pieces[s][1, t, j].reshape(32, 256)
                for r in range(2):
                    part = pl.ds(pl.multiple_of(row + (r ^ core) * PAIR, PAIR), PAIR)
                    piece = pieces[s][0, t, j, r]
                    if r == 0:
                        piece = piece * minus
                    left_ref[part, lanes] = piece
                    flip_ref[part, lanes] = piece * minus


def assembled(at, pieces):
    vm = pl.BlockSpec(memory_space=pltpu.VMEM)
    flat = jax.ShapeDtypeStruct((2 * KQ * PAIR, NG), BF)
    return pl.pallas_call(
        assemble,
        out_shape=(flat, flat, flat),
        in_specs=[pl.BlockSpec(memory_space=pltpu.SMEM)] + [vm] * 4,
        out_specs=(vm, vm, vm),
        compiler_params=pltpu.CompilerParams(vmem_limit_bytes=16 << 20),
        cost_estimate=pl.CostEstimate(flops=0, bytes_accessed=2_000_000, transcendentals=0),
    )(at, *pieces)


def stacked(w_ref, j):
    zero = jnp.zeros((BLK, BLK), BF)

    def block(b, d):
        half, i = b // 4, b % 4
        if d < 0 or d > 4 - half:
            return zero
        lane = half * SENT * BLK + d * BLK
        starts = [yh * 128 + i * 32 + zl * 16 for zl in range(2) for yh in range(4)]
        return jnp.concatenate([w_ref[at : at + 16, lane : lane + BLK] for at in starts], 0)

    first = j - 4 if j >= 4 else j - 3
    direct = jnp.concatenate(
        [
            jnp.concatenate([block(b % NB, j - b), block(b % NB, j + 1 - b)], 1)
            for b in range(first, j + 2)
        ],
        0,
    )
    width = 4 if j >= 4 else 5
    mirrored = jnp.concatenate(
        [
            jnp.concatenate([block(row, j + 1 + m - row) if j + 1 + m > row else zero for m in range(width)], 1)
            for row in (j, j + 1)
        ],
        0,
    )
    return first, direct, width, mirrored


def wrapped(x):
    return jnp.concatenate([x[:, 5 * BLK :], x, x[:, : 3 * BLK]], 1)


def screened_pair(w_ref, ahead, behind, j):
    def lanes(x, begin, count):
        return x[:, (begin + 3) * BLK : (begin + 3 + count) * BLK]

    first, direct, width, mirrored = stacked(w_ref, j)
    return nn(lanes(ahead, first, j + 2 - first), direct), nt(lanes(behind, j + 1, width), mirrored)


def contract_own(left_ref, flip_ref, own_ref, p_ref, same_ref, e1_ref, e2_ref, e3_ref):
    left, flipped = wrapped(left_ref[...]), wrapped(flip_ref[...])
    for j in range(0, NB, 2):
        fore, back = screened_pair(own_ref, left, flipped, j)
        p_ref[:, j * BLK : (j + 2) * BLK] = fore + back


    rows = left_ref.shape[0]
    half = rows // 2
    r = lax.broadcasted_iota(jnp.int32, (half, rows), 0)
    c = lax.broadcasted_iota(jnp.int32, (half, rows), 1)
    same_ref[...] = jnp.where((r >> 4) == (c >> 5), 1.0, 0.0)
    c = lax.broadcasted_iota(jnp.int32, (rows, 128), 0)
    l = lax.broadcasted_iota(jnp.int32, (rows, 128), 1)
    hit = (c & 15) == (l & 15)
    part = (c >> 4) & 1
    want = l >> 6
    e1_ref[...] = jnp.where(hit & (part == want), 1.0, 0.0)
    e2_ref[...] = jnp.where(hit & (part != want), jnp.where(want == 0, -1.0, 1.0), 0.0)
    o = lax.broadcasted_iota(jnp.int32, (4 * 8, half), 0)
    r = lax.broadcasted_iota(jnp.int32, (4 * 8, half), 1)
    e3_ref[...] = jnp.where(((r >> 4) == (o & 7)) & (((r & 15) >> 2) == (o >> 3)), 1.0, 0.0)


def contract(left_ref, flip_ref, val_ref, p_ref, same_ref, e1_ref, e2_ref, e3_ref, oth_ref, out_ref):
    rows = left_ref.shape[0]
    half = rows // 2
    left, flipped = wrapped(left_ref[...]), wrapped(flip_ref[...])
    g1 = jnp.zeros((half, rows), F32)
    g2 = jnp.zeros((half, rows), F32)
    for j in range(0, NB, 2):
        columns = slice(j * BLK, (j + 2) * BLK)
        fore, back = screened_pair(oth_ref, flipped, left, j)
        q = (fore - back).reshape(KQ, 2, PAIR, 2 * BLK)
        p = p_ref[:, columns].reshape(KQ, 2, PAIR, 2 * BLK)
        x_real = (p[:, 0] + q[:, 1]).reshape(half, 2 * BLK).astype(BF)
        x_imag = (q[:, 0] - p[:, 1]).reshape(half, 2 * BLK).astype(BF)
        val = val_ref[:, columns]
        g1 += nt(x_real, val)
        g2 += nt(x_imag, val)
    same = same_ref[...] > 0.0
    g1 = jnp.where(same, g1, 0.0)
    g2 = jnp.where(same, g2, 0.0)
    t = nn(g1, e1_ref[...], lax.Precision.HIGHEST) + nn(g2, e2_ref[...], lax.Precision.HIGHEST)
    r = lax.broadcasted_iota(jnp.int32, (half, 128), 0)
    l = lax.broadcasted_iota(jnp.int32, (half, 128), 1)
    t = jnp.where((r & 3) == ((l >> 4) & 3), t, 0.0)
    block = nn(e3_ref[...], t, lax.Precision.HIGHEST)
    for slot in range(16):
        g = slot % 4
        out_ref[slot, :, :] = block[g * 8 : g * 8 + KQ, :]


def contracted(left, flipped, val, own):
    vm = pl.BlockSpec(memory_space=pltpu.VMEM)
    kept = pltpu.CompilerParams(vmem_limit_bytes=24 << 20)
    cost = pl.CostEstimate(flops=800_000_000, bytes_accessed=2_000_000, transcendentals=0)
    oth = lax.ppermute(own, "c", [(0, 1), (1, 0)])
    shapes = ((192, NG), (96, 192), (192, 128), (192, 128), (32, 96))
    early = pl.pallas_call(
        contract_own,
        out_shape=tuple(jax.ShapeDtypeStruct(shape, F32) for shape in shapes),
        in_specs=[vm] * 3,
        out_specs=(vm,) * 5,
        compiler_params=kept,
        cost_estimate=cost,
    )(left, flipped, own)
    return pl.pallas_call(
        contract,
        out_shape=jax.ShapeDtypeStruct((16, KQ, 128), F32),
        in_specs=[vm] * 9,
        out_specs=vm,
        compiler_params=kept,
        cost_estimate=cost,
    )(left, flipped, val, *early, oth)


def pick_rows(at_ref, got_ref, pay_ref, row_ref):
    for i in range(Q * KQ):
        row = got_ref[at_ref[2 + i], pl.ds(at_ref[2 + Q * KQ + i], 1), :]
        row_ref[pl.ds(i, 1), :] = row
    pay = row_ref[...].astype(BF)
    for slot in range(32):
        pay_ref[slot, :, :] = pay


def pick_forward(at_ref, got_ref, out_ref):
    last = 2 + 2 * Q * KQ + Q
    xl, yl = at_ref[last], at_ref[last + 1]
    for q in range(Q):
        base = (q // 2) * 8 + (q % 2) * 2 + yl * 4
        for c in range(2):
            rows = got_ref[base + c, pl.ds(xl * 3, 3), :]
            out_ref[q, c * 3 : c * 3 + 3, 0, :] = rows[:, :64]
            out_ref[q, c * 3 : c * 3 + 3, 1, :] = rows[:, 64:]


def pick_back(at_ref, came_ref, out_ref):
    for q in range(Q):
        rows = came_ref[at_ref[2 + 2 * Q * KQ + q]].astype(F32)[q * KQ : (q + 1) * KQ, :]
        out_ref[q, :, 0, :] = rows[:, :64]
        out_ref[q, :, 1, :] = rows[:, 64:]


def local(cond, val, screened, k_plus):
    xl, yl, core = lax.axis_index("xl"), lax.axis_index("yl"), lax.axis_index("c")
    z, yh = lax.axis_index("z"), lax.axis_index("yh")
    w = lax.all_to_all(screened.reshape(8, 8, 256), ("xl", "xh", "c"), 0, 0)
    w = fanned((z // 2).astype(jnp.int32).reshape(1), w)
    w = lax.all_to_all(w, ("yh", "z", "yl"), 0, 0)
    own = w.reshape(NG // 2, (2 * SENT - 1) * BLK)

    x = xl * 2 + lax.axis_index("xh")

    slots = [pairs.reshape(4, 2, 3, 2, PAIR, 256) for pairs in (cond, val)]
    keep = [lax.dynamic_index_in_dim(part, core, 1, False) for part in slots]
    given = [lax.dynamic_index_in_dim(part, 1 - core, 1, False) for part in slots]
    given = jnp.stack(given, 0)
    given = lax.ppermute(given, "c", [(0, 1), (1, 0)])
    pieces = []
    for s in range(4):
        both = [
            lax.dynamic_index_in_dim(part, x ^ s, 0, False)
            for part in (keep[0], given[0], keep[1], given[1])
        ]
        piece = jnp.stack(both, 0).reshape(2, 2, 3, 2, PAIR, 256)
        if s:
            piece = lax.ppermute(piece, ("xl", "xh"), [(i, i ^ s) for i in range(4)])
        pieces.append(piece)
    corner = k_plus[:, 0]
    row_step, col_step = corner // 12, corner % 12
    here = z * 4 + yh
    other = xl ^ ((here + row_step) // 32 % 2)
    begin = (6 * yl - col_step + 12) % 12
    source = (here - row_step) % 32
    col = (begin[:, None] + jnp.arange(KQ)) % 12
    base = jnp.array([0, 2, 8, 10])[:, None]
    slot = base + col // 6 * 4 + col % 6 // 3
    row = other[:, None] * 3 + col % 3
    parts = [jnp.stack([x, core]), slot.reshape(-1), row.reshape(-1), source, jnp.stack([xl, yl])]
    at = jnp.concatenate(parts).astype(jnp.int32)
    left, flipped, right = assembled(at, pieces)
    slots = contracted(left, flipped, right, own)
    got = lax.all_to_all(slots, ("xl", "yl", "xh", "c"), 0, 0)
    vm = pl.BlockSpec(memory_space=pltpu.VMEM)
    sm = pl.BlockSpec(memory_space=pltpu.SMEM)
    out = jax.ShapeDtypeStruct((Q, KQ, 2, 64), F32)
    kept = pltpu.CompilerParams(vmem_limit_bytes=8 << 20)
    pay = pl.pallas_call(
        pick_rows,
        out_shape=jax.ShapeDtypeStruct((32, Q * KQ, 128), BF),
        in_specs=[sm, vm],
        out_specs=vm,
        scratch_shapes=[pltpu.VMEM((Q * KQ, 128), F32)],
        compiler_params=kept,
    )(at, got)
    came = lax.all_to_all(pay, ("z", "yh"), 0, 0)
    forward = pl.pallas_call(
        pick_forward, out_shape=out, in_specs=[sm, vm], out_specs=vm, compiler_params=kept
    )(at, got)
    back = pl.pallas_call(
        pick_back,
        out_shape=out,
        in_specs=[sm, vm],
        out_specs=vm,
        compiler_params=pltpu.CompilerParams(vmem_limit_bytes=8 << 20),
    )(at, came)
    return forward, back


def solution(mesh):
    fine = Mesh(mesh.devices.reshape(2, 8, 4, 2, 2, 2), ("xl", "z", "yh", "yl", "xh", "c"))
    ka, ga = ("xl", "z", "yh", "yl"), ("xh", "c")
    in_specs = (
        P(None, ka, None, None, ga),
        P(None, ka, None, None, ga),
        P(None, None, ka, ga),
        P(),
    )
    out_specs = (P(None, ka, None, ga), P(None, ka, None, ga))
    return jax.shard_map(local, mesh=fine, in_specs=in_specs, out_specs=out_specs, check_vma=False)
```

```python
import jax
import jax.numpy as jnp
from jax import lax
from jax.experimental import pallas as pl
from jax.experimental.pallas import tpu as pltpu
from jax.sharding import Mesh
from jax.sharding import PartitionSpec as P

NG = 1024
Q = 4
PAIR = 16
BLK = 128
NB = NG // BLK
SENT = 5
KQ = 6
BF = jnp.bfloat16
F32 = jnp.float32


def nt(left, right, precision=None):
    return lax.dot_general(
        left, right, (((1,), (1,)), ((), ())), preferred_element_type=F32, precision=precision
    )


def nn(left, right, precision=None):
    return jnp.dot(left, right, preferred_element_type=F32, precision=precision)


def fan(at_ref, w_ref, out_ref, piece_ref, sem):
    lane = 0
    for xl in range(2):
        for d in range(SENT - xl):
            block = lax.rem(at_ref[0] + (4 * xl + d), NB)
            lanes = pl.ds(pl.multiple_of((block % 2) * BLK, BLK), BLK)
            piece_ref[:, lane : lane + BLK] = w_ref[4 * xl + block // 2, :, lanes]
            lane += BLK
    copies = [
        pltpu.make_async_copy(piece_ref, out_ref.at[slot], sem.at[slot]) for slot in range(64)
    ]
    for copy in copies:
        copy.start()
    for copy in copies:
        copy.wait()


def fanned(at, w):
    vm = pl.BlockSpec(memory_space=pltpu.VMEM)
    return pl.pallas_call(
        fan,
        out_shape=jax.ShapeDtypeStruct((64, 8, (2 * SENT - 1) * BLK), BF),
        in_specs=[pl.BlockSpec(memory_space=pltpu.SMEM), vm],
        out_specs=pl.BlockSpec(memory_space=pl.ANY),
        scratch_shapes=[
            pltpu.VMEM((8, (2 * SENT - 1) * BLK), BF),
            pltpu.SemaphoreType.DMA((64,)),
        ],
        compiler_params=pltpu.CompilerParams(vmem_limit_bytes=16 << 20),
    )(at, w)


def assemble(at_ref, *refs):
    pieces, (left_ref, flip_ref, val_ref) = refs[:4], refs[4:]
    x, core = at_ref[0], at_ref[1]
    minus = jnp.where(core == 0, 1.0, -1.0).astype(BF)
    for s in range(4):
        xl = (x ^ s) // 2
        for t in range(2):
            g = ((x ^ s) % 2) * 2 + (core ^ t)
            lanes = pl.ds(pl.multiple_of(g * 256, 256), 256)
            for j in range(3):
                row = xl * 96 + j * 32
                whole = pl.ds(pl.multiple_of(row, 32), 32)
                val_ref[whole, lanes] = pieces[s][1, t, j].reshape(32, 256)
                for r in range(2):
                    part = pl.ds(pl.multiple_of(row + (r ^ core) * PAIR, PAIR), PAIR)
                    piece = pieces[s][0, t, j, r]
                    if r == 0:
                        piece = piece * minus
                    left_ref[part, lanes] = piece
                    flip_ref[part, lanes] = piece * minus


def assembled(at, pieces):
    vm = pl.BlockSpec(memory_space=pltpu.VMEM)
    flat = jax.ShapeDtypeStruct((2 * KQ * PAIR, NG), BF)
    return pl.pallas_call(
        assemble,
        out_shape=(flat, flat, flat),
        in_specs=[pl.BlockSpec(memory_space=pltpu.SMEM)] + [vm] * 4,
        out_specs=(vm, vm, vm),
        compiler_params=pltpu.CompilerParams(vmem_limit_bytes=16 << 20),
        cost_estimate=pl.CostEstimate(flops=0, bytes_accessed=2_000_000, transcendentals=0),
    )(at, *pieces)


def stacked(w_ref, j):
    zero = jnp.zeros((BLK, BLK), BF)

    def block(b, d):
        half, i = b // 4, b % 4
        if d < 0 or d > 4 - half:
            return zero
        lane = half * SENT * BLK + d * BLK
        starts = [yh * 128 + i * 32 + zl * 16 for zl in range(2) for yh in range(4)]
        return jnp.concatenate([w_ref[at : at + 16, lane : lane + BLK] for at in starts], 0)

    first = j - 4 if j >= 4 else j - 3
    direct = jnp.concatenate(
        [
            jnp.concatenate([block(b % NB, j - b), block(b % NB, j + 1 - b)], 1)
            for b in range(first, j + 2)
        ],
        0,
    )
    width = 4 if j >= 4 else 5
    mirrored = jnp.concatenate(
        [
            jnp.concatenate([block(row, j + 1 + m - row) if j + 1 + m > row else zero for m in range(width)], 1)
            for row in (j, j + 1)
        ],
        0,
    )
    return first, direct, width, mirrored


def wrapped(x):
    return jnp.concatenate([x[:, 5 * BLK :], x, x[:, : 3 * BLK]], 1)


def screened_pair(w_ref, ahead, behind, j):
    def lanes(x, begin, count):
        return x[:, (begin + 3) * BLK : (begin + 3 + count) * BLK]

    first, direct, width, mirrored = stacked(w_ref, j)
    return nn(lanes(ahead, first, j + 2 - first), direct), nt(lanes(behind, j + 1, width), mirrored)


def contract_own(left_ref, flip_ref, own_ref, p_ref):
    left, flipped = wrapped(left_ref[...]), wrapped(flip_ref[...])
    for j in range(0, NB, 2):
        fore, back = screened_pair(own_ref, left, flipped, j)
        p_ref[:, j * BLK : (j + 2) * BLK] = fore + back


def contract(left_ref, flip_ref, val_ref, p_ref, oth_ref, out_ref):
    rows = left_ref.shape[0]
    half = rows // 2
    left, flipped = wrapped(left_ref[...]), wrapped(flip_ref[...])
    g1 = jnp.zeros((half, rows), F32)
    g2 = jnp.zeros((half, rows), F32)
    for j in range(0, NB, 2):
        columns = slice(j * BLK, (j + 2) * BLK)
        fore, back = screened_pair(oth_ref, flipped, left, j)
        q = (fore - back).reshape(KQ, 2, PAIR, 2 * BLK)
        p = p_ref[:, columns].reshape(KQ, 2, PAIR, 2 * BLK)
        x_real = (p[:, 0] + q[:, 1]).reshape(half, 2 * BLK).astype(BF)
        x_imag = (q[:, 0] - p[:, 1]).reshape(half, 2 * BLK).astype(BF)
        val = val_ref[:, columns]
        g1 += nt(x_real, val)
        g2 += nt(x_imag, val)
    r = lax.broadcasted_iota(jnp.int32, (half, rows), 0)
    c = lax.broadcasted_iota(jnp.int32, (half, rows), 1)
    same = r // PAIR == c // (2 * PAIR)
    g1 = jnp.where(same, g1, 0.0)
    g2 = jnp.where(same, g2, 0.0)
    c = lax.broadcasted_iota(jnp.int32, (rows, 128), 0)
    l = lax.broadcasted_iota(jnp.int32, (rows, 128), 1)
    hit = c % PAIR == l % PAIR
    part = (c // PAIR) % 2
    want = l // 64
    e1 = jnp.where(hit & (part == want), 1.0, 0.0)
    e2 = jnp.where(hit & (part != want), jnp.where(want == 0, -1.0, 1.0), 0.0)
    t = nn(g1, e1, lax.Precision.HIGHEST) + nn(g2, e2, lax.Precision.HIGHEST)
    r = lax.broadcasted_iota(jnp.int32, (half, 128), 0)
    l = lax.broadcasted_iota(jnp.int32, (half, 128), 1)
    t = jnp.where(r % 4 == (l // PAIR) % 4, t, 0.0)
    o = lax.broadcasted_iota(jnp.int32, (4 * 8, half), 0)
    r = lax.broadcasted_iota(jnp.int32, (4 * 8, half), 1)
    e3 = jnp.where((r // PAIR == o % 8) & ((r % PAIR) // 4 == o // 8), 1.0, 0.0)
    block = nn(e3, t, lax.Precision.HIGHEST)
    for slot in range(16):
        g = slot % 4
        out_ref[slot, :, :] = block[g * 8 : g * 8 + KQ, :]


def contracted(left, flipped, val, own):
    vm = pl.BlockSpec(memory_space=pltpu.VMEM)
    kept = pltpu.CompilerParams(vmem_limit_bytes=24 << 20)
    cost = pl.CostEstimate(flops=800_000_000, bytes_accessed=2_000_000, transcendentals=0)
    oth = lax.ppermute(own, "c", [(0, 1), (1, 0)])
    p = pl.pallas_call(
        contract_own,
        out_shape=jax.ShapeDtypeStruct((2 * KQ * PAIR, NG), F32),
        in_specs=[vm] * 3,
        out_specs=vm,
        compiler_params=kept,
        cost_estimate=cost,
    )(left, flipped, own)
    return pl.pallas_call(
        contract,
        out_shape=jax.ShapeDtypeStruct((16, KQ, 128), F32),
        in_specs=[vm] * 5,
        out_specs=vm,
        compiler_params=kept,
        cost_estimate=cost,
    )(left, flipped, val, p, oth)


def pick_rows(at_ref, got_ref, pay_ref, row_ref):
    for i in range(Q * KQ):
        row = got_ref[at_ref[2 + i], pl.ds(at_ref[2 + Q * KQ + i], 1), :]
        row_ref[pl.ds(i, 1), :] = row
    pay = row_ref[...].astype(BF)
    for slot in range(32):
        pay_ref[slot, :, :] = pay


def pick_forward(at_ref, got_ref, out_ref):
    last = 2 + 2 * Q * KQ + Q
    xl, yl = at_ref[last], at_ref[last + 1]
    for q in range(Q):
        base = (q // 2) * 8 + (q % 2) * 2 + yl * 4
        for c in range(2):
            rows = got_ref[base + c, pl.ds(xl * 3, 3), :]
            out_ref[q, c * 3 : c * 3 + 3, 0, :] = rows[:, :64]
            out_ref[q, c * 3 : c * 3 + 3, 1, :] = rows[:, 64:]


def pick_back(at_ref, came_ref, out_ref):
    for q in range(Q):
        rows = came_ref[at_ref[2 + 2 * Q * KQ + q]].astype(F32)[q * KQ : (q + 1) * KQ, :]
        out_ref[q, :, 0, :] = rows[:, :64]
        out_ref[q, :, 1, :] = rows[:, 64:]


def local(cond, val, screened, k_plus):
    xl, yl, core = lax.axis_index("xl"), lax.axis_index("yl"), lax.axis_index("c")
    z, yh = lax.axis_index("z"), lax.axis_index("yh")
    w = lax.all_to_all(screened.reshape(8, 8, 256), ("xl", "xh", "c"), 0, 0)
    w = fanned((z // 2).astype(jnp.int32).reshape(1), w)
    w = lax.all_to_all(w, ("yh", "z", "yl"), 0, 0)
    own = w.reshape(NG // 2, (2 * SENT - 1) * BLK)

    x = xl * 2 + lax.axis_index("xh")

    slots = [pairs.reshape(4, 2, 3, 2, PAIR, 256) for pairs in (cond, val)]
    keep = [lax.dynamic_index_in_dim(part, core, 1, False) for part in slots]
    given = [lax.dynamic_index_in_dim(part, 1 - core, 1, False) for part in slots]
    given = jnp.stack(given, 0)
    given = lax.ppermute(given, "c", [(0, 1), (1, 0)])
    pieces = []
    for s in range(4):
        both = [
            lax.dynamic_index_in_dim(part, x ^ s, 0, False)
            for part in (keep[0], given[0], keep[1], given[1])
        ]
        piece = jnp.stack(both, 0).reshape(2, 2, 3, 2, PAIR, 256)
        if s:
            piece = lax.ppermute(piece, ("xl", "xh"), [(i, i ^ s) for i in range(4)])
        pieces.append(piece)
    corner = k_plus[:, 0]
    row_step, col_step = corner // 12, corner % 12
    here = z * 4 + yh
    other = xl ^ ((here + row_step) // 32 % 2)
    begin = (6 * yl - col_step + 12) % 12
    source = (here - row_step) % 32
    col = (begin[:, None] + jnp.arange(KQ)) % 12
    base = jnp.array([0, 2, 8, 10])[:, None]
    slot = base + col // 6 * 4 + col % 6 // 3
    row = other[:, None] * 3 + col % 3
    parts = [jnp.stack([x, core]), slot.reshape(-1), row.reshape(-1), source, jnp.stack([xl, yl])]
    at = jnp.concatenate(parts).astype(jnp.int32)
    left, flipped, right = assembled(at, pieces)
    slots = contracted(left, flipped, right, own)
    got = lax.all_to_all(slots, ("xl", "yl", "xh", "c"), 0, 0)
    vm = pl.BlockSpec(memory_space=pltpu.VMEM)
    sm = pl.BlockSpec(memory_space=pltpu.SMEM)
    out = jax.ShapeDtypeStruct((Q, KQ, 2, 64), F32)
    kept = pltpu.CompilerParams(vmem_limit_bytes=8 << 20)
    pay = pl.pallas_call(
        pick_rows,
        out_shape=jax.ShapeDtypeStruct((32, Q * KQ, 128), BF),
        in_specs=[sm, vm],
        out_specs=vm,
        scratch_shapes=[pltpu.VMEM((Q * KQ, 128), F32)],
        compiler_params=kept,
    )(at, got)
    came = lax.all_to_all(pay, ("z", "yh"), 0, 0)
    forward = pl.pallas_call(
        pick_forward, out_shape=out, in_specs=[sm, vm], out_specs=vm, compiler_params=kept
    )(at, got)
    back = pl.pallas_call(
        pick_back,
        out_shape=out,
        in_specs=[sm, vm],
        out_specs=vm,
        compiler_params=pltpu.CompilerParams(vmem_limit_bytes=8 << 20),
    )(at, came)
    return forward, back


def solution(mesh):
    fine = Mesh(mesh.devices.reshape(2, 8, 4, 2, 2, 2), ("xl", "z", "yh", "yl", "xh", "c"))
    ka, ga = ("xl", "z", "yh", "yl"), ("xh", "c")
    in_specs = (
        P(None, ka, None, None, ga),
        P(None, ka, None, None, ga),
        P(None, None, ka, ga),
        P(),
    )
    out_specs = (P(None, ka, None, ga), P(None, ka, None, ga))
    return jax.shard_map(local, mesh=fine, in_specs=in_specs, out_specs=out_specs, check_vma=False)
```
